512 devices in a mesh: ctx: 64 (over y_hi, z, core), head: 8 (over x, y_lo).
Axes of the slice: x: 4, y: 4 (y_hi: 2, y_lo: 2; y = y_hi * 2 + y_lo), z: 16, core: 2. Of those that a mesh axis runs over, the one named last changes fastest.
Arguments:
- clean_latents: bfloat16 [128, 4, 8, 128], P('ctx'), may hold values from -6 to 6
- noise: bfloat16 [128, 4, 8, 128], P('ctx'), may hold values from -6 to 6
- timesteps: int32 [128], P('ctx'), may hold values from 0 to 999
- span_order: int32 [128], P('ctx'), may hold values from 0 to 127, as said below
- valid_frames: int32 [128], P('ctx'), may hold values from 1 to 4
- embed_weight: bfloat16 [256, 6144], P(None, 'head'), may hold values from -0.375 to 0.375
- position: bfloat16 [8192, 6144], P('ctx'), may hold values from -6 to 6
- norm_gain: bfloat16 [6144], replicated, may hold values from 0.099609375 to 1.8984375
- query_weight: bfloat16 [6144, 3072], P('ctx', 'head'), as said below
- kv_weight: bfloat16 [6144, 2048], P('ctx', 'head'), as said below
Outputs:
- attended: bfloat16 [8192, 3072], P('ctx', 'head')
The draws below stay inside these ranges and needn't reach their ends.
Inputs may be any that keep to these rules, and one draw needn't show every extreme that they name: `span_order`: span slots 2d and 2d + 1 hold spans p and 127 - p for some p, in either order; each span number stands once. `query_weight`: entries scale with the fan-in 6144. `kv_weight`: entries scale with the fan-in 6144.
All inputs are finite; a program needn't handle non-finite values.
Results may differ from the reference program's by a relative error of at most 0.012.
The reference program's roundings to bfloat16 on the way count: a program that leaves them out, or rounds other values in their place, can miss the bound.
Values may be sent and summed in bfloat16 or wider, within the bound.
No kernel may reach another device: no remote copies, remote signals or barrier semaphores. Data moves between devices by JAX's collectives and lax.ppermute only.
A program may use at most 64 MiB of HBM per device.

```python
import jax
import jax.numpy as jnp
from jax import lax

D = 6144
HD = 128
KVH = 8
GROUP = 3
CH = 16
FR = 4
PH = 4
PW = 4
QHEADS = 24
PATCH = 256
LH = 8
LW = 8
CT = 64
SPANS = 128


def draw_query_weight(key, part):
    fresh = jax.random.normal(jax.random.fold_in(key, 12), (D, KVH, GROUP, HD), jnp.float32)
    values = 3.0 * fresh
    return (values * D ** (-0.5)).reshape(D, KVH * GROUP * HD).astype(jnp.bfloat16)


def draw_kv_weight(key, part):
    fresh_keys = jax.random.normal(jax.random.fold_in(key, 13), (D, KVH, HD), jnp.float32)
    fresh_values = jax.random.normal(jax.random.fold_in(key, 14), (D, KVH, HD), jnp.float32)
    key_part = fresh_keys
    stacked = jnp.stack([key_part, fresh_values], axis=2)
    return (stacked * D ** (-0.5)).reshape(D, KVH * 2 * HD).astype(jnp.bfloat16)


def draw_span_order(key, part):
    pairs = SPANS // 2
    chosen = jax.random.permutation(jax.random.fold_in(key, 21), pairs).astype(jnp.int32)
    flipped = jax.random.randint(jax.random.fold_in(key, 22), (pairs,), 0, 2).astype(jnp.int32)
    mirror = SPANS - 1 - chosen
    first_slot = jnp.where(flipped == 1, mirror, chosen)
    second_slot = jnp.where(flipped == 1, chosen, mirror)
    return jnp.stack([first_slot, second_slot], axis=1).reshape(SPANS).astype(jnp.int32)


def draw_valid_frames(key, part):
    counts = jax.random.randint(jax.random.fold_in(key, 31), (SPANS,), 1, FR + 1).astype(jnp.int32)
    full_slot = jax.random.randint(jax.random.fold_in(key, 32), (), 0, SPANS).astype(jnp.int32)
    short_slot = (full_slot + 1 + jax.random.randint(jax.random.fold_in(key, 33), (), 0, SPANS - 1)) % SPANS
    positions = jnp.arange(SPANS, dtype=jnp.int32)
    counts = jnp.where(positions == full_slot, FR, counts)
    counts = jnp.where(positions == short_slot, 1, counts)
    return counts.astype(jnp.int32)


def place_ends(values, key, smallest, high):
    index_at = [jax.random.randint(jax.random.fold_in(key, axis), (), 0, length) for axis, length in enumerate(values.shape)]
    widest = values.shape.index(max(values.shape))
    beside = index_at[:widest] + [(index_at[widest] + 1) % values.shape[widest]] + index_at[widest + 1:]
    return values.at[tuple(index_at)].set(smallest).at[tuple(beside)].set(high)


def steps_of(key, shape, cuts, low, high):
    def one(dim, shards_of):
        draws = jax.random.uniform(jax.random.fold_in(jax.random.fold_in(key, 6), dim), (shards_of,), jnp.float32, low / len(cuts), high / len(cuts))
        return jnp.repeat(jnp.exp(draws), shape[dim] // shards_of).reshape((-1,) + (1,) * (len(shape) - dim - 1))

    level = one(*cuts[0])
    for cut in cuts[1:]:
        level = level * one(*cut)
    return level


def bell_draw(rng, shape, deviation, limit, cuts=(), kind=jnp.bfloat16):
    drawn = jax.random.normal(rng, shape, jnp.float32) * deviation
    if len(cuts) > 0:
        drawn = steps_of(rng, shape, cuts, -0.22, 0.18) * drawn
    return jnp.clip(drawn, min=-limit, max=limit).astype(kind)


def setup_inputs(seed: int = 0) -> dict:
    seeds = jax.random.split(jax.random.key(seed), 11)
    clean_latents = bell_draw(seeds[0], (SPANS, FR, LH, LW * CH), 1.0, 6.0, ((0, 64),))
    noise = bell_draw(seeds[1], (SPANS, FR, LH, LW * CH), 1.0, 6.0, ((0, 64),))
    timesteps = place_ends(jax.random.randint(seeds[2], (SPANS,), 0, 1000), jax.random.fold_in(seeds[2], 1), 0, 999).astype(jnp.int32)
    span_order = draw_span_order(jax.random.fold_in(seeds[10], 71), 0)
    valid_frames = draw_valid_frames(jax.random.fold_in(seeds[10], 71), 0)
    embed_weight = bell_draw(seeds[5], (PATCH, D), PATCH ** -0.5, 0.375, ((1, 8),))
    position = bell_draw(seeds[6], (SPANS * CT, D), 1.0, 6.0, ((0, 64),))
    norm_gain = jnp.clip(1.0 + 0.18 * jax.random.normal(seeds[7], (D,), jnp.float32), 0.099609375, 1.8984375).astype(jnp.bfloat16)
    query_weight = draw_query_weight(jax.random.fold_in(seeds[10], 71), 0)
    kv_weight = draw_kv_weight(jax.random.fold_in(seeds[10], 71), 0)
    return dict(clean_latents=clean_latents, noise=noise, timesteps=timesteps, span_order=span_order, valid_frames=valid_frames, embed_weight=embed_weight, position=position, norm_gain=norm_gain, query_weight=query_weight, kv_weight=kv_weight)


eps_norm = 1e-06
masked_low = -1e+30

def make_patches(latents):
    slots, frames, height, flat = latents.shape
    width = flat // CH
    grid = latents.reshape(slots, frames, height, width, CH)
    padded = jnp.pad(grid, ((0, 0), (0, 0), (1, 1), (1, 1), (0, 0)))
    half_rows = height // 2
    half_cols = width // 2
    split = padded.reshape(slots, frames, half_rows + 1, 2, half_cols + 1, 2, CH)
    offsets_list = []
    for row_off in range(4):
        for col_off in range(4):
            offsets_list.append(split[:, :, row_off // 2:row_off // 2 + half_rows, row_off % 2, col_off // 2:col_off // 2 + half_cols, col_off % 2, :])
    stacked = jnp.stack(offsets_list, axis=4)
    return stacked.reshape(slots * frames * half_rows * half_cols, 16 * CH)

def rms_normalize(values, gain):
    wide = values.astype(jnp.float32)
    factor = lax.rsqrt(lax.optimization_barrier(jnp.mean(wide * wide, axis=-1, keepdims=True)) + eps_norm)
    return (wide * factor * gain.astype(jnp.float32)).astype(jnp.bfloat16)

def reference(clean_latents, noise, timesteps, span_order, valid_frames, embed_weight, position, norm_gain, query_weight, kv_weight):
    level = ((timesteps.astype(jnp.float32) + 1.0) / 1000.0)[:, None, None, None]
    noisy_latents = ((1.0 - level) * clean_latents.astype(jnp.float32) + level * noise.astype(jnp.float32)).astype(jnp.bfloat16)

    def embed_tokens(latents):
        projected = jnp.dot(make_patches(latents), embed_weight, preferred_element_type=jnp.float32)
        embedded = (projected + position.astype(jnp.float32)).astype(jnp.bfloat16)
        return rms_normalize(embedded, norm_gain)
    normed_noisy = embed_tokens(noisy_latents)
    normed_clean = embed_tokens(clean_latents)
    queries = jnp.dot(normed_noisy, query_weight, preferred_element_type=jnp.float32).astype(jnp.bfloat16)
    noisy_kv = jnp.dot(normed_noisy, kv_weight, preferred_element_type=jnp.float32).astype(jnp.bfloat16)
    clean_kv = jnp.dot(normed_clean, kv_weight, preferred_element_type=jnp.float32).astype(jnp.bfloat16)
    frame_rows = PH * PW
    frame_of_row = jnp.arange(CT, dtype=jnp.int32) // frame_rows
    clean_span = jnp.repeat(span_order, CT)
    clean_live = jnp.tile(frame_of_row, SPANS) < jnp.repeat(valid_frames, CT)
    score_scale = HD ** (-0.5)

    def one_slot(slot):
        first = (slot * CT).astype(jnp.int32)
        query_block = lax.dynamic_slice_in_dim(queries, first, CT, 0).reshape(CT, KVH, GROUP, HD).astype(jnp.float32)
        own_block = lax.dynamic_slice_in_dim(noisy_kv, first, CT, 0)
        own_live = frame_of_row < valid_frames[slot]
        allowed = jnp.concatenate([own_live, clean_live & (clean_span < span_order[slot])])
        blocks = jnp.concatenate([own_block, clean_kv], axis=0).reshape(-1, KVH, 2, HD).astype(jnp.float32)
        scores = jnp.einsum('tkgd,nkd->tkgn', query_block, blocks[:, :, 0]) * score_scale
        lowered = jnp.where(allowed, scores, masked_low)
        largest = lax.optimization_barrier(jnp.max(lowered, axis=-1, keepdims=True))
        raw = jnp.where(allowed, jnp.exp(lowered - largest), 0.0)
        total = lax.optimization_barrier(jnp.sum(raw, axis=-1))
        weights = lax.optimization_barrier(raw.astype(jnp.bfloat16)).astype(jnp.float32)
        summed = jnp.einsum('tkgn,nkd->tkgd', weights, blocks[:, :, 1]) / total[..., None]
        summed = jnp.where(own_live[:, None, None, None], summed, 0.0)
        return summed.reshape(CT, QHEADS * HD).astype(jnp.bfloat16)
    result = lax.map(one_slot, jnp.arange(SPANS, dtype=jnp.int32))
    return result.reshape(SPANS * CT, QHEADS * HD)
```

```python
import math

import jax
import jax.numpy as jnp
from jax import lax
from jax.experimental import pallas as pl
from jax.experimental.pallas import tpu as pltpu
from jax.sharding import Mesh, PartitionSpec as P

HD = 128
CH = 16


eps_norm = 1e-06
masked_low = -1e30


def make_patches(latents):
    slots, frames, height, flat = latents.shape
    width = flat // CH
    grid = latents.reshape(slots, frames, height, width, CH)
    padded = jnp.pad(grid, ((0, 0), (0, 0), (1, 1), (1, 1), (0, 0)))
    half_rows = height // 2
    half_cols = width // 2
    split = padded.reshape(slots, frames, half_rows + 1, 2, half_cols + 1, 2, CH)
    offsets_list = []
    for row_off in range(4):
        for col_off in range(4):
            offsets_list.append(
                split[
                    :,
                    :,
                    row_off // 2 : row_off // 2 + half_rows,
                    row_off % 2,
                    col_off // 2 : col_off // 2 + half_cols,
                    col_off % 2,
                    :,
                ]
            )
    stacked = jnp.stack(offsets_list, axis=4)
    return stacked.reshape(slots * frames * half_rows * half_cols, 16 * CH)


def rms_normalize(values, gain):
    wide = values.astype(jnp.float32)
    factor = lax.rsqrt(jnp.mean(wide * wide, axis=-1, keepdims=True) + eps_norm)
    return (wide * factor * gain.astype(jnp.float32)).astype(jnp.bfloat16)


CTX = ("yh", "z", "core")
HEAD = ("x", "yl")
meta_rows = 16
score_factor = HD ** (-0.5) * math.log2(math.e)
key_chunk = 1024


def attention_kernel(valid_ref, q_ref, own_ref, kv_ref, bias_ref, out_ref):
    tokens = q_ref.shape[0]
    group = q_ref.shape[1] // HD
    span_rows = tokens // 2
    frame_rows = span_rows // 4
    q = jnp.concatenate([q_ref[:, g * HD : (g + 1) * HD] for g in range(group)], axis=0)

    def scores_of(keys, bias):
        s = lax.dot_general(q, keys, (((1,), (1,)), ((), ())), preferred_element_type=jnp.float32)
        s = s.reshape(group, tokens, keys.shape[0]) * score_factor + bias[None]
        return s.reshape(group * tokens, keys.shape[0])

    row = lax.broadcasted_iota(jnp.int32, (tokens, tokens), 0)
    col = lax.broadcasted_iota(jnp.int32, (tokens, tokens), 1)
    valid_col = jnp.where(col < span_rows, valid_ref[0], valid_ref[1])
    same = (row < span_rows) == (col < span_rows)
    live_col = lax.rem(col, span_rows) < valid_col * frame_rows
    own_bias = jnp.where(same & live_col, 0.0, masked_low)
    s = scores_of(own_ref[:, :HD], own_bias)
    largest = jnp.max(s, axis=1, keepdims=True)
    raw = jnp.exp2(s - largest)
    total = jnp.sum(raw, axis=1, keepdims=True)
    summed = jnp.dot(raw.astype(jnp.bfloat16), own_ref[:, HD:], preferred_element_type=jnp.float32)
    first = lax.broadcasted_iota(jnp.int32, (tokens, key_chunk), 0) < span_rows
    for start in range(0, kv_ref.shape[0], key_chunk):
        keys = kv_ref[start : start + key_chunk, :HD]
        values = kv_ref[start : start + key_chunk, HD:]
        bias = jnp.where(
            first,
            bias_ref[0:1, start : start + key_chunk],
            bias_ref[1:2, start : start + key_chunk],
        )
        s = scores_of(keys, bias)
        new_largest = jnp.maximum(largest, jnp.max(s, axis=1, keepdims=True))
        raw = jnp.exp2(s - new_largest)
        factor = jnp.exp2(largest - new_largest)
        total = total * factor + jnp.sum(raw, axis=1, keepdims=True)
        summed = summed * factor + jnp.dot(
            raw.astype(jnp.bfloat16), values, preferred_element_type=jnp.float32
        )
        largest = new_largest
    result = summed / total
    token = lax.broadcasted_iota(jnp.int32, (tokens, HD), 0)
    valid_row = jnp.where(token < span_rows, valid_ref[0], valid_ref[1])
    live_row = lax.rem(token, span_rows) < valid_row * frame_rows
    for g in range(group):
        piece = result[g * tokens : (g + 1) * tokens]
        out_ref[:, g * HD : (g + 1) * HD] = jnp.where(live_row, piece, 0.0).astype(jnp.bfloat16)


def attention(valid, q, own, kv_all, bias):
    vmem = pl.BlockSpec(memory_space=pltpu.VMEM)
    return pl.pallas_call(
        attention_kernel,
        out_shape=jax.ShapeDtypeStruct(q.shape, jnp.bfloat16),
        in_specs=[pl.BlockSpec(memory_space=pltpu.SMEM), vmem, vmem, vmem, vmem],
        out_specs=vmem,
        compiler_params=pltpu.CompilerParams(vmem_limit_bytes=40 * 1024 * 1024),
    )(valid, q, own, kv_all, bias)


def add_position(projected, position_rows, tokens):
    cols = projected.shape[1]
    doubled = projected.reshape(2, tokens, cols) + position_rows.astype(jnp.float32)[None]
    return doubled.reshape(2 * tokens, cols).astype(jnp.bfloat16)


def on_device(
    clean_latents,
    noise,
    timesteps,
    span_order,
    valid_frames,
    embed_weight,
    position,
    norm_gain,
    query_weight,
    kv_weight,
):
    slots, frames, height, flat = clean_latents.shape
    frame_rows = height // 2 * (flat // (2 * CH))
    span_rows = frames * frame_rows
    tokens = slots * span_rows
    core = lax.axis_index("core")
    half = embed_weight.shape[0] // 2
    own_embed = lax.all_gather(
        lax.dynamic_slice_in_dim(embed_weight, core * half, half, 0), HEAD, axis=1, tiled=True
    )
    rows, kv_cols = kv_weight.shape
    meta = jnp.concatenate([span_order, valid_frames]).astype(jnp.float16)
    meta_block = jnp.pad(meta[None, :], ((0, meta_rows - 1), (0, kv_cols - 2 * slots)))
    kv_shard = jnp.concatenate([kv_weight.astype(jnp.float16), meta_block], axis=0)
    kv_pair = lax.all_gather(kv_shard, "yh", axis=0, tiled=True)
    kv_gathered = lax.all_gather(kv_pair, ("z", "core"), axis=0, tiled=True)
    kv_gathered = kv_gathered.reshape(-1, 2, rows + meta_rows, kv_cols)
    kv_full = kv_gathered[:, :, :rows].swapaxes(0, 1).astype(jnp.bfloat16).reshape(-1, kv_cols)
    meta_all = kv_gathered[:, :, rows, : 2 * slots].astype(jnp.float32).astype(jnp.int32)
    q_pair = lax.all_gather(query_weight, "yh", axis=0, tiled=True)
    q_gathered = lax.all_gather(q_pair, ("z", "core"), axis=0, tiled=True)
    q_gathered = q_gathered.reshape(-1, 2, rows, query_weight.shape[1])

    other_embed = lax.ppermute(own_embed, "core", [(0, 1), (1, 0)])
    level = ((timesteps.astype(jnp.float32) + 1.0) / 1000.0)[:, None, None, None]
    noisy_latents = (
        (1.0 - level) * clean_latents.astype(jnp.float32) + level * noise.astype(jnp.float32)
    ).astype(jnp.bfloat16)
    patches = make_patches(jnp.concatenate([noisy_latents, clean_latents], axis=0))
    own_patches = lax.dynamic_slice_in_dim(patches, core * half, half, 1)
    other_patches = lax.dynamic_slice_in_dim(patches, (1 - core) * half, half, 1)
    projected = jnp.dot(
        own_patches, own_embed, preferred_element_type=jnp.float32
    ) + jnp.dot(other_patches, other_embed, preferred_element_type=jnp.float32)
    embedded = add_position(projected, position, tokens)
    normed = rms_normalize(embedded, norm_gain)
    keys_values = jnp.dot(normed, kv_full, preferred_element_type=jnp.float32).astype(jnp.bfloat16)

    clean_pair = lax.all_gather(keys_values[tokens:].astype(jnp.float16), "yh", axis=0, tiled=True)
    kv_all = lax.all_gather(clean_pair, ("z", "core"), axis=0, tiled=True).astype(jnp.bfloat16)

    key_order = meta_all[:, :, :slots].reshape(-1)
    key_valid = meta_all[:, :, slots:].reshape(-1)
    frame = jnp.arange(span_rows, dtype=jnp.int32) // frame_rows
    live = (frame[None, :] < key_valid[:, None])[None]
    earlier = (key_order[None, :] < span_order[:, None])[:, :, None]
    bias = jnp.where(live & earlier, 0.0, masked_low).reshape(slots, -1)

    pairs = q_gathered.shape[0]
    normed_noisy = normed[:tokens].reshape(tokens, 2, pairs * rows)
    queries = jnp.dot(
        normed_noisy[:, 0], q_gathered[:, 0].reshape(pairs * rows, -1), preferred_element_type=jnp.float32
    ) + jnp.dot(
        normed_noisy[:, 1], q_gathered[:, 1].reshape(pairs * rows, -1), preferred_element_type=jnp.float32
    )
    return attention(
        valid_frames, queries.astype(jnp.bfloat16), keys_values[:tokens], kv_all, bias
    )


def solution(mesh):
    fine = Mesh(mesh.devices.reshape(2, 16, 2, 4, 2), CTX + HEAD)
    return jax.shard_map(
        on_device,
        mesh=fine,
        in_specs=(
            P(CTX, None, None, None),
            P(CTX, None, None, None),
            P(CTX),
            P(CTX),
            P(CTX),
            P(None, HEAD),
            P(CTX, None),
            P(),
            P(CTX, HEAD),
            P(CTX, HEAD),
        ),
        out_specs=P(CTX, HEAD),
        check_vma=False,
    )
```

```python
import math

import jax
import jax.numpy as jnp
from jax import lax
from jax.experimental import pallas as pl
from jax.experimental.pallas import tpu as pltpu
from jax.sharding import Mesh, PartitionSpec as P

HD = 128
CH = 16


eps_norm = 1e-06
masked_low = -1e30


def patch_kernel(core_ref, time_ref, clean_ref, noise_ref, own_ref, other_ref):
    rows, lanes = clean_ref.shape
    row = lax.broadcasted_iota(jnp.int32, (rows, lanes), 0)
    steps = jnp.where(row < rows // 2, time_ref[0], time_ref[1])
    level = (steps.astype(jnp.float32) + 1.0) / 1000.0
    clean = clean_ref[...]
    noisy = (
        (1.0 - level) * clean.astype(jnp.float32) + level * noise_ref[...].astype(jnp.float32)
    ).astype(jnp.bfloat16)
    latents = jnp.concatenate([noisy, clean], axis=0)
    count = 2 * rows
    source = lax.broadcasted_iota(jnp.int32, (lanes, 256), 0)
    target = lax.broadcasted_iota(jnp.int32, (lanes, 256), 1)
    token = lax.broadcasted_iota(jnp.int32, (256, 4 * count), 0)
    place = lax.broadcasted_iota(jnp.int32, (256, 4 * count), 1)
    result = jnp.zeros((256, 256), jnp.float32)
    for kernel_row in range(4):
        shifted = []
        for token_col in range(4):
            wanted = (target & 63) + (32 * token_col - 16)
            pick = (source == wanted) & ((target >> 6) == kernel_row)
            pick = jnp.where(pick, 1.0, 0.0).astype(jnp.bfloat16)
            shifted.append(
                jnp.dot(latents, pick, preferred_element_type=jnp.float32).astype(jnp.bfloat16)
            )
        latent_row = 2 * ((token >> 2) & 3) - 1 + kernel_row
        wanted = (token & 3) * count + (token >> 4) * 8 + latent_row
        pick = (place == wanted) & (latent_row >= 0) & (latent_row < 8)
        pick = jnp.where(pick, 1.0, 0.0).astype(jnp.bfloat16)
        result += jnp.dot(pick, jnp.concatenate(shifted, axis=0), preferred_element_type=jnp.float32)
    patches = result.astype(jnp.bfloat16)
    half = patches.shape[1] // 2
    upper = core_ref[0] == 1
    own_ref[...] = jnp.where(upper, patches[:, half:], patches[:, :half])
    other_ref[...] = jnp.where(upper, patches[:, :half], patches[:, half:])


def make_patches(core, timesteps, clean_latents, noise):
    flat = clean_latents.shape[-1]
    smem = pl.BlockSpec(memory_space=pltpu.SMEM)
    vmem = pl.BlockSpec(memory_space=pltpu.VMEM)
    shape = jax.ShapeDtypeStruct((256, 128), jnp.bfloat16)
    return pl.pallas_call(
        patch_kernel,
        out_shape=(shape, shape),
        in_specs=[smem, smem, vmem, vmem],
        out_specs=(vmem, vmem),
    )(core[None], timesteps, clean_latents.reshape(-1, flat), noise.reshape(-1, flat))


def rms_normalize(values, gain):
    wide = values.astype(jnp.float32)
    factor = lax.rsqrt(jnp.mean(wide * wide, axis=-1, keepdims=True) + eps_norm)
    return (wide * factor * gain.astype(jnp.float32)).astype(jnp.bfloat16)


CTX = ("yh", "z", "core")
HEAD = ("x", "yl")
meta_rows = 16
score_factor = HD ** (-0.5) * math.log2(math.e)
key_chunk = 1024


def attention_kernel(valid_ref, q_ref, own_ref, kv_ref, bias_ref, out_ref):
    tokens = q_ref.shape[0]
    group = q_ref.shape[1] // HD
    span_rows = tokens // 2
    frame_rows = span_rows // 4
    q = jnp.concatenate([q_ref[:, g * HD : (g + 1) * HD] for g in range(group)], axis=0)

    def scores_of(keys, bias):
        s = lax.dot_general(q, keys, (((1,), (1,)), ((), ())), preferred_element_type=jnp.float32)
        s = s.reshape(group, tokens, keys.shape[0]) * score_factor + bias[None]
        return s.reshape(group * tokens, keys.shape[0])

    row = lax.broadcasted_iota(jnp.int32, (tokens, tokens), 0)
    col = lax.broadcasted_iota(jnp.int32, (tokens, tokens), 1)
    valid_col = jnp.where(col < span_rows, valid_ref[0], valid_ref[1])
    same = (row < span_rows) == (col < span_rows)
    live_col = lax.rem(col, span_rows) < valid_col * frame_rows
    own_bias = jnp.where(same & live_col, 0.0, masked_low)
    s = scores_of(own_ref[:, :HD], own_bias)
    largest = jnp.max(s, axis=1, keepdims=True)
    raw = jnp.exp2(s - largest)
    total = jnp.sum(raw, axis=1, keepdims=True)
    summed = jnp.dot(raw.astype(jnp.bfloat16), own_ref[:, HD:], preferred_element_type=jnp.float32)
    first = lax.broadcasted_iota(jnp.int32, (tokens, key_chunk), 0) < span_rows
    for start in range(0, kv_ref.shape[0], key_chunk):
        keys = kv_ref[start : start + key_chunk, :HD]
        values = kv_ref[start : start + key_chunk, HD:]
        bias = jnp.where(
            first,
            bias_ref[0:1, start : start + key_chunk],
            bias_ref[1:2, start : start + key_chunk],
        )
        s = scores_of(keys, bias)
        new_largest = jnp.maximum(largest, jnp.max(s, axis=1, keepdims=True))
        raw = jnp.exp2(s - new_largest)
        factor = jnp.exp2(largest - new_largest)
        total = total * factor + jnp.sum(raw, axis=1, keepdims=True)
        summed = summed * factor + jnp.dot(
            raw.astype(jnp.bfloat16), values, preferred_element_type=jnp.float32
        )
        largest = new_largest
    result = summed / total
    token = lax.broadcasted_iota(jnp.int32, (tokens, HD), 0)
    valid_row = jnp.where(token < span_rows, valid_ref[0], valid_ref[1])
    live_row = lax.rem(token, span_rows) < valid_row * frame_rows
    for g in range(group):
        piece = result[g * tokens : (g + 1) * tokens]
        out_ref[:, g * HD : (g + 1) * HD] = jnp.where(live_row, piece, 0.0).astype(jnp.bfloat16)


def attention(valid, q, own, kv_all, bias):
    vmem = pl.BlockSpec(memory_space=pltpu.VMEM)
    return pl.pallas_call(
        attention_kernel,
        out_shape=jax.ShapeDtypeStruct(q.shape, jnp.bfloat16),
        in_specs=[pl.BlockSpec(memory_space=pltpu.SMEM), vmem, vmem, vmem, vmem],
        out_specs=vmem,
        compiler_params=pltpu.CompilerParams(vmem_limit_bytes=24 * 1024 * 1024),
    )(valid, q, own, kv_all, bias)


def add_position(projected, position_rows, tokens):
    cols = projected.shape[1]
    doubled = projected.reshape(2, tokens, cols) + position_rows.astype(jnp.float32)[None]
    return doubled.reshape(2 * tokens, cols).astype(jnp.bfloat16)


def on_device(
    clean_latents,
    noise,
    timesteps,
    span_order,
    valid_frames,
    embed_weight,
    position,
    norm_gain,
    query_weight,
    kv_weight,
):
    slots, frames, height, flat = clean_latents.shape
    frame_rows = height // 2 * (flat // (2 * CH))
    span_rows = frames * frame_rows
    tokens = slots * span_rows
    core = lax.axis_index("core")
    half = embed_weight.shape[0] // 2
    own_embed = lax.all_gather(
        lax.dynamic_slice_in_dim(embed_weight, core * half, half, 0), HEAD, axis=1, tiled=True
    )
    rows, kv_cols = kv_weight.shape
    q_cols = query_weight.shape[1]
    weights = jnp.concatenate([query_weight, kv_weight], axis=1).astype(jnp.float16)
    meta = jnp.concatenate([span_order, valid_frames]).astype(jnp.float16)
    meta_block = jnp.pad(meta[None, :], ((0, meta_rows - 1), (q_cols, kv_cols - 2 * slots)))
    weights_pair = lax.all_gather(jnp.concatenate([weights, meta_block], axis=0), "yh", axis=0)
    kv_gathered = lax.all_gather(
        weights_pair[:, :, q_cols:], ("z", "core"), axis=1, tiled=True
    ).reshape(-1, rows + meta_rows, kv_cols)
    kv_full = kv_gathered[:, :rows].astype(jnp.bfloat16).reshape(-1, kv_cols)
    meta_all = kv_gathered[:, rows, : 2 * slots].astype(jnp.float32).astype(jnp.int32)
    q_full = lax.all_gather(
        weights_pair[:, :rows, :q_cols].astype(jnp.bfloat16), ("z", "core"), axis=1, tiled=True
    ).reshape(-1, q_cols)

    other_embed = lax.ppermute(own_embed, "core", [(0, 1), (1, 0)])
    own_patches, other_patches = make_patches(core, timesteps, clean_latents, noise)
    projected = jnp.dot(
        own_patches, own_embed, preferred_element_type=jnp.float32
    ) + jnp.dot(other_patches, other_embed, preferred_element_type=jnp.float32)
    embedded = add_position(projected, position, tokens)
    normed = rms_normalize(embedded, norm_gain)
    keys_values = jnp.dot(normed, kv_full, preferred_element_type=jnp.float32).astype(jnp.bfloat16)

    clean_pair = lax.all_gather(keys_values[tokens:].astype(jnp.float16), "yh", axis=0)
    kv_all = (
        lax.all_gather(clean_pair, ("z", "core"), axis=1, tiled=True)
        .reshape(-1, kv_cols)
        .astype(jnp.bfloat16)
    )

    key_order = meta_all[:, :slots].reshape(-1)
    key_valid = meta_all[:, slots:].reshape(-1)
    frame = jnp.arange(span_rows, dtype=jnp.int32) // frame_rows
    live = (frame[None, :] < key_valid[:, None])[None]
    earlier = (key_order[None, :] < span_order[:, None])[:, :, None]
    bias = jnp.where(live & earlier, 0.0, masked_low).reshape(slots, -1)

    queries = jnp.dot(normed[:tokens], q_full, preferred_element_type=jnp.float32)
    return attention(
        valid_frames, queries.astype(jnp.bfloat16), keys_values[:tokens], kv_all, bias
    )


def solution(mesh):
    fine = Mesh(mesh.devices.reshape(2, 16, 2, 4, 2), CTX + HEAD)
    return jax.shard_map(
        on_device,
        mesh=fine,
        in_specs=(
            P(CTX, None, None, None),
            P(CTX, None, None, None),
            P(CTX),
            P(CTX),
            P(CTX),
            P(None, HEAD),
            P(CTX, None),
            P(),
            P(CTX, HEAD),
            P(CTX, HEAD),
        ),
        out_specs=P(CTX, HEAD),
        check_vma=False,
    )
```

```python
import math

import jax
import jax.numpy as jnp
from jax import lax
from jax.experimental import pallas as pl
from jax.experimental.pallas import tpu as pltpu
from jax.sharding import Mesh, PartitionSpec as P

HD = 128
CH = 16


eps_norm = 1e-06
masked_low = -1e30


def in_hbm(array):
    return pltpu.with_memory_space_constraint(array, pltpu.HBM)


def patch_kernel(core_ref, time_ref, clean_ref, noise_ref, after_ref, own_ref, other_ref):
    del after_ref
    rows, lanes = clean_ref.shape
    row = lax.broadcasted_iota(jnp.int32, (rows, lanes), 0)
    steps = jnp.where(row < rows // 2, time_ref[0], time_ref[1])
    level = (steps.astype(jnp.float32) + 1.0) / 1000.0
    clean = clean_ref[...]
    noisy = (
        (1.0 - level) * clean.astype(jnp.float32) + level * noise_ref[...].astype(jnp.float32)
    ).astype(jnp.bfloat16)
    latents = jnp.concatenate([noisy, clean], axis=0)
    count = 2 * rows
    source = lax.broadcasted_iota(jnp.int32, (lanes, 256), 0)
    target = lax.broadcasted_iota(jnp.int32, (lanes, 256), 1)
    token = lax.broadcasted_iota(jnp.int32, (256, 4 * count), 0)
    place = lax.broadcasted_iota(jnp.int32, (256, 4 * count), 1)
    result = jnp.zeros((256, 256), jnp.float32)
    for kernel_row in range(4):
        shifted = []
        for token_col in range(4):
            wanted = (target & 63) + (32 * token_col - 16)
            pick = (source == wanted) & ((target >> 6) == kernel_row)
            pick = jnp.where(pick, 1.0, 0.0).astype(jnp.bfloat16)
            shifted.append(
                jnp.dot(latents, pick, preferred_element_type=jnp.float32).astype(jnp.bfloat16)
            )
        latent_row = 2 * ((token >> 2) & 3) - 1 + kernel_row
        wanted = (token & 3) * count + (token >> 4) * 8 + latent_row
        pick = (place == wanted) & (latent_row >= 0) & (latent_row < 8)
        pick = jnp.where(pick, 1.0, 0.0).astype(jnp.bfloat16)
        result += jnp.dot(pick, jnp.concatenate(shifted, axis=0), preferred_element_type=jnp.float32)
    patches = result.astype(jnp.bfloat16)
    half = patches.shape[1] // 2
    upper = core_ref[0] == 1
    own_ref[...] = jnp.where(upper, patches[:, half:], patches[:, :half])
    other_ref[...] = jnp.where(upper, patches[:, :half], patches[:, half:])


def make_patches(core, timesteps, clean_latents, noise, after):
    flat = clean_latents.shape[-1]
    smem = pl.BlockSpec(memory_space=pltpu.SMEM)
    vmem = pl.BlockSpec(memory_space=pltpu.VMEM)
    shape = jax.ShapeDtypeStruct((256, 128), jnp.bfloat16)
    return pl.pallas_call(
        patch_kernel,
        out_shape=(shape, shape),
        in_specs=[smem, smem, vmem, vmem, pl.BlockSpec(memory_space=pltpu.HBM)],
        out_specs=(vmem, vmem),
        compiler_params=pltpu.CompilerParams(vmem_limit_bytes=8 * 1024 * 1024),
    )(core[None], timesteps, clean_latents.reshape(-1, flat), noise.reshape(-1, flat), in_hbm(after))


CTX = ("yh", "z", "core")
HEAD = ("x", "yl")
meta_rows = 16
score_factor = HD ** (-0.5) * math.log2(math.e)
key_chunk = 1024
column_chunk = 768
weight_pieces = 6
embed_pieces = 4


def attention_kernel(
    valid_ref,
    normed_ref,
    weight_ref,
    own_ref,
    kv_first_ref,
    kv_second_ref,
    bias_ref,
    out_ref,
    normed_buffer,
    buffer_ref,
    normed_sems,
    sems,
):
    tokens, width = normed_ref.shape
    group = weight_ref.shape[1] // HD
    depth = width // weight_pieces
    copies = []
    for piece in range(weight_pieces):
        rows = pl.ds(piece * depth, depth)
        copies.append(
            (
                pltpu.make_async_copy(
                    normed_ref.at[:, rows], normed_buffer.at[:, rows], normed_sems.at[piece]
                ),
                pltpu.make_async_copy(weight_ref.at[rows], buffer_ref.at[rows], sems.at[piece]),
            )
        )
        for copy in copies[-1]:
            copy.start()
    span_rows = tokens // 2
    frame_rows = span_rows // 4
    queries = jnp.zeros((tokens, weight_ref.shape[1]), jnp.float32)
    for piece in range(weight_pieces):
        for copy in copies[piece]:
            copy.wait()
        span = slice(piece * depth, (piece + 1) * depth)
        queries += jnp.dot(
            normed_buffer[:, span], buffer_ref[span, :], preferred_element_type=jnp.float32
        )
    queries = queries.astype(jnp.bfloat16)
    q = jnp.concatenate([queries[:, g * HD : (g + 1) * HD] for g in range(group)], axis=0)

    def scores_of(keys, bias):
        s = lax.dot_general(q, keys, (((1,), (1,)), ((), ())), preferred_element_type=jnp.float32)
        s = s.reshape(group, tokens, keys.shape[0]) * score_factor + bias[None]
        return s.reshape(group * tokens, keys.shape[0])

    row = lax.broadcasted_iota(jnp.int32, (tokens, tokens), 0)
    col = lax.broadcasted_iota(jnp.int32, (tokens, tokens), 1)
    valid_col = jnp.where(col < span_rows, valid_ref[0], valid_ref[1])
    same = (row < span_rows) == (col < span_rows)
    live_col = lax.rem(col, span_rows) < valid_col * frame_rows
    own_bias = jnp.where(same & live_col, 0.0, masked_low)
    s = scores_of(own_ref[:, :HD], own_bias)
    largest = jnp.max(s, axis=1, keepdims=True)
    raw = jnp.exp2(s - largest)
    total = jnp.sum(raw, axis=1, keepdims=True)
    summed = jnp.dot(raw.astype(jnp.bfloat16), own_ref[:, HD:], preferred_element_type=jnp.float32)
    first = lax.broadcasted_iota(jnp.int32, (tokens, key_chunk), 0) < span_rows
    key_rows = kv_first_ref.shape[0]
    for start in range(0, 2 * key_rows, key_chunk):
        kv_ref = kv_first_ref if start < key_rows else kv_second_ref
        inside = start % key_rows
        keys = kv_ref[inside : inside + key_chunk, :HD]
        values = kv_ref[inside : inside + key_chunk, HD:]
        bias = jnp.where(
            first,
            bias_ref[0:1, start : start + key_chunk],
            bias_ref[1:2, start : start + key_chunk],
        )
        s = scores_of(keys, bias)
        new_largest = jnp.maximum(largest, jnp.max(s, axis=1, keepdims=True))
        raw = jnp.exp2(s - new_largest)
        factor = jnp.exp2(largest - new_largest)
        total = total * factor + jnp.sum(raw, axis=1, keepdims=True)
        summed = summed * factor + jnp.dot(
            raw.astype(jnp.bfloat16), values, preferred_element_type=jnp.float32
        )
        largest = new_largest
    result = summed / total
    token = lax.broadcasted_iota(jnp.int32, (tokens, HD), 0)
    valid_row = jnp.where(token < span_rows, valid_ref[0], valid_ref[1])
    live_row = lax.rem(token, span_rows) < valid_row * frame_rows
    for g in range(group):
        piece = result[g * tokens : (g + 1) * tokens]
        out_ref[:, g * HD : (g + 1) * HD] = jnp.where(live_row, piece, 0.0).astype(jnp.bfloat16)


def attention(valid, normed, weight, own, kv_first, kv_second, bias):
    vmem = pl.BlockSpec(memory_space=pltpu.VMEM)
    hbm = pl.BlockSpec(memory_space=pltpu.HBM)
    return pl.pallas_call(
        attention_kernel,
        out_shape=jax.ShapeDtypeStruct((normed.shape[0], weight.shape[1]), jnp.bfloat16),
        in_specs=[
            pl.BlockSpec(memory_space=pltpu.SMEM),
            hbm,
            hbm,
            vmem,
            vmem,
            vmem,
            vmem,
        ],
        out_specs=vmem,
        scratch_shapes=[
            pltpu.VMEM(normed.shape, jnp.bfloat16),
            pltpu.VMEM(weight.shape, jnp.bfloat16),
            pltpu.SemaphoreType.DMA((weight_pieces,)),
            pltpu.SemaphoreType.DMA((weight_pieces,)),
        ],
        compiler_params=pltpu.CompilerParams(vmem_limit_bytes=20 * 1024 * 1024),
    )(valid, in_hbm(normed), in_hbm(weight), own, kv_first, kv_second, bias)


def embed_kernel(
    own_patch_ref,
    other_patch_ref,
    own_embed_ref,
    other_embed_ref,
    position_ref,
    gain_ref,
    weight_ref,
    normed_ref,
    noisy_ref,
    clean_ref,
    embedded_ref,
    own_buffer,
    position_buffer,
    sems,
    out_sems,
):
    tokens, width = position_ref.shape
    piece_cols = width // embed_pieces
    copies = []
    for piece in range(embed_pieces):
        cols = pl.ds(piece * piece_cols, piece_cols)
        for index, (source, buffer) in enumerate(
            (
                (own_embed_ref, own_buffer),
                (position_ref, position_buffer),
            )
        ):
            copies.append(
                pltpu.make_async_copy(source.at[:, cols], buffer.at[:, cols], sems.at[index, piece])
            )
            copies[-1].start()
    patches = jnp.concatenate([own_patch_ref[...], other_patch_ref[...]], axis=1)
    squares = jnp.zeros((2 * tokens, 1), jnp.float32)
    for start in range(0, width, column_chunk):
        cols = slice(start, start + column_chunk)
        if start % piece_cols == 0:
            first = 2 * (start // piece_cols)
            for copy in copies[first : first + 2]:
                copy.wait()
        embed = jnp.concatenate([own_buffer[:, cols], other_embed_ref[:, cols]], axis=0)
        projected = jnp.dot(patches, embed, preferred_element_type=jnp.float32)
        place = position_buffer[:, cols].astype(jnp.float32)
        embedded = (projected + jnp.concatenate([place, place], axis=0)).astype(jnp.bfloat16)
        embedded_ref[:, cols] = embedded
        wide = embedded.astype(jnp.float32)
        squares += jnp.sum(wide * wide, axis=1, keepdims=True)
    factor = lax.rsqrt(squares / width + eps_norm)
    summed = jnp.zeros((2 * tokens, weight_ref.shape[1]), jnp.float32)
    stores = []
    for start in range(0, width, column_chunk):
        cols = slice(start, start + column_chunk)
        wide = embedded_ref[:, cols].astype(jnp.float32)
        normed = (wide * factor * gain_ref[:, cols].astype(jnp.float32)).astype(jnp.bfloat16)
        embedded_ref[:tokens, cols] = normed[:tokens]
        if (start + column_chunk) % piece_cols == 0:
            piece = start // piece_cols
            done = pl.ds(piece * piece_cols, piece_cols)
            stores.append(
                pltpu.make_async_copy(
                    embedded_ref.at[:tokens, done], normed_ref.at[:, done], out_sems.at[piece]
                )
            )
            stores[-1].start()
        summed += jnp.dot(normed, weight_ref[cols, :], preferred_element_type=jnp.float32)
    noisy_ref[...] = summed[:tokens].astype(jnp.bfloat16)
    clean_ref[...] = summed[tokens:].astype(jnp.bfloat16)
    for store in stores:
        store.wait()


def embed_tokens(own_patches, other_patches, own_embed, other_embed, position, gain, weight):
    tokens, width = position.shape
    vmem = pl.BlockSpec(memory_space=pltpu.VMEM)
    hbm = pl.BlockSpec(memory_space=pltpu.HBM)
    kv_shape = jax.ShapeDtypeStruct((tokens, weight.shape[1]), jnp.bfloat16)
    return pl.pallas_call(
        embed_kernel,
        out_shape=(jax.ShapeDtypeStruct((tokens, width), jnp.bfloat16), kv_shape, kv_shape),
        in_specs=[vmem, vmem, hbm, vmem, hbm, vmem, vmem],
        out_specs=(hbm, vmem, vmem),
        scratch_shapes=[
            pltpu.VMEM((2 * tokens, width), jnp.bfloat16),
            pltpu.VMEM(own_embed.shape, jnp.bfloat16),
            pltpu.VMEM(position.shape, jnp.bfloat16),
            pltpu.SemaphoreType.DMA((2, embed_pieces)),
            pltpu.SemaphoreType.DMA((embed_pieces,)),
        ],
        compiler_params=pltpu.CompilerParams(vmem_limit_bytes=24 * 1024 * 1024),
    )(
        own_patches,
        other_patches,
        in_hbm(own_embed),
        other_embed,
        in_hbm(position),
        gain[None],
        weight,
    )


def on_device(
    clean_latents,
    noise,
    timesteps,
    span_order,
    valid_frames,
    embed_weight,
    position,
    norm_gain,
    query_weight,
    kv_weight,
):
    slots, frames, height, flat = clean_latents.shape
    frame_rows = height // 2 * (flat // (2 * CH))
    span_rows = frames * frame_rows
    tokens = slots * span_rows
    core = lax.axis_index("core")
    half = embed_weight.shape[0] // 2
    own_embed = lax.all_gather(
        lax.dynamic_slice_in_dim(embed_weight, core * half, half, 0), HEAD, axis=1, tiled=True
    )
    rows, kv_cols = kv_weight.shape
    q_cols = query_weight.shape[1]
    weights = jnp.concatenate([query_weight, kv_weight], axis=1).astype(jnp.float16)
    meta = jnp.concatenate([span_order, valid_frames]).astype(jnp.float16)
    meta_block = jnp.pad(meta[None, :], ((0, meta_rows - 1), (q_cols, kv_cols - 2 * slots)))
    weights_pair = lax.all_gather(jnp.concatenate([weights, meta_block], axis=0), "yh", axis=0)
    kv_gathered = lax.all_gather(
        weights_pair[:, :, q_cols:], ("z", "core"), axis=1, tiled=True
    ).reshape(-1, rows + meta_rows, kv_cols)
    kv_full = kv_gathered[:, :rows].astype(jnp.bfloat16).reshape(-1, kv_cols)
    meta_all = kv_gathered[:, rows, : 2 * slots].astype(jnp.float32).astype(jnp.int32)
    q_full = lax.all_gather(
        weights_pair[:, :rows, :q_cols].astype(jnp.bfloat16), ("z", "core"), axis=1, tiled=True
    ).reshape(-1, q_cols)

    other_embed = lax.ppermute(own_embed, "core", [(0, 1), (1, 0)])
    own_patches, other_patches = make_patches(core, timesteps, clean_latents, noise, own_embed)
    normed_noisy, noisy_kv, clean_kv = embed_tokens(
        own_patches, other_patches, own_embed, other_embed, position, norm_gain, kv_full
    )

    clean_pair = lax.all_gather(clean_kv.astype(jnp.float16), "yh", axis=0)
    clean_all = lax.all_gather(clean_pair, ("z", "core"), axis=1, tiled=True)
    kv_first = clean_all[0].astype(jnp.bfloat16)
    kv_second = clean_all[1].astype(jnp.bfloat16)

    key_order = meta_all[:, :slots].reshape(-1)
    key_valid = meta_all[:, slots:].reshape(-1)
    frame = jnp.arange(span_rows, dtype=jnp.int32) // frame_rows
    live = (frame[None, :] < key_valid[:, None])[None]
    earlier = (key_order[None, :] < span_order[:, None])[:, :, None]
    bias = jnp.where(live & earlier, 0.0, masked_low).reshape(slots, -1)

    return attention(valid_frames, normed_noisy, q_full, noisy_kv, kv_first, kv_second, bias)


def solution(mesh):
    fine = Mesh(mesh.devices.reshape(2, 16, 2, 4, 2), CTX + HEAD)
    return jax.shard_map(
        on_device,
        mesh=fine,
        in_specs=(
            P(CTX, None, None, None),
            P(CTX, None, None, None),
            P(CTX),
            P(CTX),
            P(CTX),
            P(None, HEAD),
            P(CTX, None),
            P(),
            P(CTX, HEAD),
            P(CTX, HEAD),
        ),
        out_specs=P(CTX, HEAD),
        check_vma=False,
    )
```

```python
import math

import jax
import jax.numpy as jnp
from jax import lax
from jax.experimental import pallas as pl
from jax.experimental.pallas import tpu as pltpu
from jax.sharding import Mesh, PartitionSpec as P

HD = 128
CH = 16


eps_norm = 1e-06
masked_low = -1e30


def in_hbm(array):
    return pltpu.with_memory_space_constraint(array, pltpu.HBM)


def patch_kernel(
    scalar_ref, clean_hbm, noise_hbm, after_ref, own_ref, other_ref, clean_ref, noise_ref, sems
):
    del after_ref
    loads = [
        pltpu.make_async_copy(clean_hbm, clean_ref, sems.at[0]),
        pltpu.make_async_copy(noise_hbm, noise_ref, sems.at[1]),
    ]
    for load in loads:
        load.start()
    rows, lanes = clean_ref.shape
    row = lax.broadcasted_iota(jnp.int32, (rows, lanes), 0)
    steps = jnp.where(row < rows // 2, scalar_ref[1], scalar_ref[2])
    level = (steps.astype(jnp.float32) + 1.0) / 1000.0
    for load in loads:
        load.wait()
    clean = clean_ref[...]
    noisy = (
        (1.0 - level) * clean.astype(jnp.float32) + level * noise_ref[...].astype(jnp.float32)
    ).astype(jnp.bfloat16)
    latents = jnp.concatenate([noisy, clean], axis=0)
    count = 2 * rows
    source = lax.broadcasted_iota(jnp.int32, (lanes, 256), 0)
    target = lax.broadcasted_iota(jnp.int32, (lanes, 256), 1)
    token = lax.broadcasted_iota(jnp.int32, (256, 4 * count), 0)
    place = lax.broadcasted_iota(jnp.int32, (256, 4 * count), 1)
    result = jnp.zeros((256, 256), jnp.float32)
    for kernel_row in range(4):
        shifted = []
        for token_col in range(4):
            wanted = (target & 63) + (32 * token_col - 16)
            pick = (source == wanted) & ((target >> 6) == kernel_row)
            pick = jnp.where(pick, 1.0, 0.0).astype(jnp.bfloat16)
            shifted.append(
                jnp.dot(latents, pick, preferred_element_type=jnp.float32).astype(jnp.bfloat16)
            )
        latent_row = 2 * ((token >> 2) & 3) - 1 + kernel_row
        wanted = (token & 3) * count + (token >> 4) * 8 + latent_row
        pick = (place == wanted) & (latent_row >= 0) & (latent_row < 8)
        pick = jnp.where(pick, 1.0, 0.0).astype(jnp.bfloat16)
        result += jnp.dot(pick, jnp.concatenate(shifted, axis=0), preferred_element_type=jnp.float32)
    patches = result.astype(jnp.bfloat16)
    half = patches.shape[1] // 2
    upper = scalar_ref[0] == 1
    own_ref[...] = jnp.where(upper, patches[:, half:], patches[:, :half])
    other_ref[...] = jnp.where(upper, patches[:, :half], patches[:, half:])


def make_patches(scalars, clean_latents, noise, after):
    flat = clean_latents.shape[-1]
    rows = clean_latents.size // flat
    hbm = pl.BlockSpec(memory_space=pltpu.HBM)
    vmem = pl.BlockSpec(memory_space=pltpu.VMEM)
    shape = jax.ShapeDtypeStruct((256, 128), jnp.bfloat16)
    return pl.pallas_call(
        patch_kernel,
        out_shape=(shape, shape),
        in_specs=[pl.BlockSpec(memory_space=pltpu.SMEM), hbm, hbm, hbm],
        out_specs=(vmem, vmem),
        scratch_shapes=[
            pltpu.VMEM((rows, flat), jnp.bfloat16),
            pltpu.VMEM((rows, flat), jnp.bfloat16),
            pltpu.SemaphoreType.DMA((2,)),
        ],
        compiler_params=pltpu.CompilerParams(vmem_limit_bytes=8 * 1024 * 1024),
    )(
        scalars,
        in_hbm(clean_latents.reshape(rows, flat)),
        in_hbm(noise.reshape(rows, flat)),
        in_hbm(after),
    )


CTX = ("yh", "z", "core")
HEAD = ("x", "yl")
meta_rows = 16
score_factor = HD ** (-0.5) * math.log2(math.e)
key_chunk = 1024
column_chunk = 768
weight_pieces = 6
embed_pieces = 4


def attention_kernel(
    scalar_ref,
    normed_ref,
    weight_ref,
    own_ref,
    kv_hbm,
    meta_ref,
    out_ref,
    normed_buffer,
    buffer_ref,
    kv_ref,
    normed_sems,
    sems,
    kv_sems,
):
    orders = (scalar_ref[3], scalar_ref[4])
    valids = (scalar_ref[5], scalar_ref[6])
    tokens, width = normed_ref.shape
    group = weight_ref.shape[1] // HD
    depth = width // weight_pieces
    copies = []
    for piece in range(weight_pieces):
        rows = pl.ds(piece * depth, depth)
        copies.append(
            (
                pltpu.make_async_copy(
                    normed_ref.at[:, rows], normed_buffer.at[:, rows], normed_sems.at[piece]
                ),
                pltpu.make_async_copy(weight_ref.at[rows], buffer_ref.at[rows], sems.at[piece]),
            )
        )
        for copy in copies[-1]:
            copy.start()
    span_rows = tokens // 2
    frame_rows = span_rows // 4
    kv_copies = []
    for piece in range(kv_ref.shape[0] // key_chunk):
        rows = pl.ds(piece * key_chunk, key_chunk)
        kv_copies.append(
            pltpu.make_async_copy(kv_hbm.at[rows], kv_ref.at[rows], kv_sems.at[piece])
        )
        kv_copies[-1].start()
    meta = meta_ref[...].astype(jnp.bfloat16)
    blocks = meta.shape[0]
    block_row = lax.broadcasted_iota(jnp.int32, (blocks, key_chunk), 0)
    block_col = lax.broadcasted_iota(jnp.int32, (blocks, key_chunk), 1)
    key_place = lax.broadcasted_iota(jnp.int32, (1, key_chunk), 1)
    second = (key_place & span_rows) != 0
    key_frame = ((key_place & (span_rows - 1)) // frame_rows).astype(jnp.float32)
    biases = []
    for piece in range(kv_ref.shape[0] // key_chunk):
        pick = block_row == ((block_col + piece * key_chunk) // tokens)
        spread = lax.dot_general(
            meta,
            jnp.where(pick, 1.0, 0.0).astype(jnp.bfloat16),
            (((0,), (0,)), ((), ())),
            preferred_element_type=jnp.float32,
        )
        key_order = jnp.where(second, spread[1:2], spread[0:1])
        key_valid = jnp.where(second, spread[3:4], spread[2:3])
        live = key_frame < key_valid
        biases.append(
            [
                jnp.where(live & (key_order < order.astype(jnp.float32)), 0.0, masked_low)
                for order in orders
            ]
        )
    queries = jnp.zeros((tokens, weight_ref.shape[1]), jnp.float32)
    for piece in range(weight_pieces):
        for copy in copies[piece]:
            copy.wait()
        span = slice(piece * depth, (piece + 1) * depth)
        queries += jnp.dot(
            normed_buffer[:, span], buffer_ref[span, :], preferred_element_type=jnp.float32
        )
    queries = queries.astype(jnp.bfloat16)
    q = jnp.concatenate([queries[:, g * HD : (g + 1) * HD] for g in range(group)], axis=0)

    def scores_of(keys, bias):
        s = lax.dot_general(q, keys, (((1,), (1,)), ((), ())), preferred_element_type=jnp.float32)
        s = s.reshape(group, tokens, keys.shape[0]) * score_factor + bias[None]
        return s.reshape(group * tokens, keys.shape[0])

    row = lax.broadcasted_iota(jnp.int32, (tokens, tokens), 0)
    col = lax.broadcasted_iota(jnp.int32, (tokens, tokens), 1)
    valid_col = jnp.where(col < span_rows, valids[0], valids[1])
    same = (row < span_rows) == (col < span_rows)
    live_col = lax.rem(col, span_rows) < valid_col * frame_rows
    own_bias = jnp.where(same & live_col, 0.0, masked_low)
    s = scores_of(own_ref[:, :HD], own_bias)
    largest = jnp.max(s, axis=1, keepdims=True)
    raw = jnp.exp2(s - largest)
    total = jnp.sum(raw, axis=1, keepdims=True)
    summed = jnp.dot(raw.astype(jnp.bfloat16), own_ref[:, HD:], preferred_element_type=jnp.float32)
    first = lax.broadcasted_iota(jnp.int32, (tokens, key_chunk), 0) < span_rows
    for start in range(0, kv_ref.shape[0], key_chunk):
        kv_copies[start // key_chunk].wait()
        keys = kv_ref[start : start + key_chunk, :HD]
        values = kv_ref[start : start + key_chunk, HD:]
        bias = jnp.where(first, biases[start // key_chunk][0], biases[start // key_chunk][1])
        s = scores_of(keys, bias)
        new_largest = jnp.maximum(largest, jnp.max(s, axis=1, keepdims=True))
        raw = jnp.exp2(s - new_largest)
        factor = jnp.exp2(largest - new_largest)
        total = total * factor + jnp.sum(raw, axis=1, keepdims=True)
        summed = summed * factor + jnp.dot(
            raw.astype(jnp.bfloat16), values, preferred_element_type=jnp.float32
        )
        largest = new_largest
    result = summed / total
    token = lax.broadcasted_iota(jnp.int32, (tokens, HD), 0)
    valid_row = jnp.where(token < span_rows, valids[0], valids[1])
    live_row = lax.rem(token, span_rows) < valid_row * frame_rows
    for g in range(group):
        piece = result[g * tokens : (g + 1) * tokens]
        out_ref[:, g * HD : (g + 1) * HD] = jnp.where(live_row, piece, 0.0).astype(jnp.bfloat16)


def attention(scalars, normed, weight, own, kv_all, meta):
    smem = pl.BlockSpec(memory_space=pltpu.SMEM)
    vmem = pl.BlockSpec(memory_space=pltpu.VMEM)
    hbm = pl.BlockSpec(memory_space=pltpu.HBM)
    return pl.pallas_call(
        attention_kernel,
        out_shape=jax.ShapeDtypeStruct((normed.shape[0], weight.shape[1]), jnp.bfloat16),
        in_specs=[smem, hbm, hbm, vmem, hbm, vmem],
        out_specs=vmem,
        scratch_shapes=[
            pltpu.VMEM(normed.shape, jnp.bfloat16),
            pltpu.VMEM(weight.shape, jnp.bfloat16),
            pltpu.VMEM(kv_all.shape, jnp.bfloat16),
            pltpu.SemaphoreType.DMA((weight_pieces,)),
            pltpu.SemaphoreType.DMA((weight_pieces,)),
            pltpu.SemaphoreType.DMA((kv_all.shape[0] // key_chunk,)),
        ],
        compiler_params=pltpu.CompilerParams(vmem_limit_bytes=32 * 1024 * 1024),
    )(scalars, in_hbm(normed), in_hbm(weight), own, in_hbm(kv_all), meta)


def embed_kernel(
    own_patch_ref,
    other_patch_ref,
    own_embed_ref,
    other_embed_ref,
    position_ref,
    gain_ref,
    weight_ref,
    normed_ref,
    noisy_ref,
    clean_ref,
    embedded_ref,
    own_buffer,
    position_buffer,
    sems,
    out_sems,
):
    tokens, width = position_ref.shape
    piece_cols = width // embed_pieces
    copies = []
    for piece in range(embed_pieces):
        cols = pl.ds(piece * piece_cols, piece_cols)
        for index, (source, buffer) in enumerate(
            (
                (own_embed_ref, own_buffer),
                (position_ref, position_buffer),
            )
        ):
            copies.append(
                pltpu.make_async_copy(source.at[:, cols], buffer.at[:, cols], sems.at[index, piece])
            )
            copies[-1].start()
    patches = jnp.concatenate([own_patch_ref[...], other_patch_ref[...]], axis=1)
    squares = jnp.zeros((2 * tokens, 128), jnp.float32)
    for start in range(0, width, column_chunk):
        cols = slice(start, start + column_chunk)
        if start % piece_cols == 0:
            first = 2 * (start // piece_cols)
            for copy in copies[first : first + 2]:
                copy.wait()
        embed = jnp.concatenate([own_buffer[:, cols], other_embed_ref[:, cols]], axis=0)
        projected = jnp.dot(patches, embed, preferred_element_type=jnp.float32)
        place = position_buffer[:, cols].astype(jnp.float32)
        embedded = (projected + jnp.concatenate([place, place], axis=0)).astype(jnp.bfloat16)
        embedded_ref[:, cols] = embedded
        wide = embedded.astype(jnp.float32)
        for lane in range(0, column_chunk, 128):
            squares += wide[:, lane : lane + 128] * wide[:, lane : lane + 128]
    factor = lax.rsqrt(jnp.sum(squares, axis=1, keepdims=True) / width + eps_norm)
    summed = jnp.zeros((2 * tokens, weight_ref.shape[1]), jnp.float32)
    stores = []
    for start in range(0, width, column_chunk):
        cols = slice(start, start + column_chunk)
        wide = embedded_ref[:, cols].astype(jnp.float32)
        normed = (wide * factor * gain_ref[:, cols].astype(jnp.float32)).astype(jnp.bfloat16)
        embedded_ref[:tokens, cols] = normed[:tokens]
        if (start + column_chunk) % piece_cols == 0:
            piece = start // piece_cols
            done = pl.ds(piece * piece_cols, piece_cols)
            stores.append(
                pltpu.make_async_copy(
                    embedded_ref.at[:tokens, done], normed_ref.at[:, done], out_sems.at[piece]
                )
            )
            stores[-1].start()
        summed += jnp.dot(normed, weight_ref[cols, :], preferred_element_type=jnp.float32)
    noisy_ref[...] = summed[:tokens].astype(jnp.bfloat16)
    clean_ref[...] = summed[tokens:].astype(jnp.bfloat16)
    for store in stores:
        store.wait()


def embed_tokens(own_patches, other_patches, own_embed, other_embed, position, gain, weight):
    tokens, width = position.shape
    vmem = pl.BlockSpec(memory_space=pltpu.VMEM)
    hbm = pl.BlockSpec(memory_space=pltpu.HBM)
    kv_shape = jax.ShapeDtypeStruct((tokens, weight.shape[1]), jnp.bfloat16)
    return pl.pallas_call(
        embed_kernel,
        out_shape=(pltpu.HBM((tokens, width), jnp.bfloat16), kv_shape, kv_shape),
        in_specs=[vmem, vmem, hbm, vmem, hbm, vmem, vmem],
        out_specs=(hbm, vmem, vmem),
        scratch_shapes=[
            pltpu.VMEM((2 * tokens, width), jnp.bfloat16),
            pltpu.VMEM(own_embed.shape, jnp.bfloat16),
            pltpu.VMEM(position.shape, jnp.bfloat16),
            pltpu.SemaphoreType.DMA((2, embed_pieces)),
            pltpu.SemaphoreType.DMA((embed_pieces,)),
        ],
        compiler_params=pltpu.CompilerParams(vmem_limit_bytes=24 * 1024 * 1024),
    )(
        own_patches,
        other_patches,
        in_hbm(own_embed),
        other_embed,
        in_hbm(position),
        gain[None],
        weight,
    )


def on_device(
    clean_latents,
    noise,
    timesteps,
    span_order,
    valid_frames,
    embed_weight,
    position,
    norm_gain,
    query_weight,
    kv_weight,
):
    slots = clean_latents.shape[0]
    core = lax.axis_index("core")
    half = embed_weight.shape[0] // 2
    scalars = in_hbm(jnp.concatenate([core[None], timesteps, span_order, valid_frames]))
    own_embed = lax.all_gather(
        lax.dynamic_slice_in_dim(embed_weight, core * half, half, 0), HEAD, axis=1, tiled=True
    )
    rows, kv_cols = kv_weight.shape
    q_cols = query_weight.shape[1]
    weights = jnp.concatenate([query_weight, kv_weight], axis=1).astype(jnp.float16)
    meta = jnp.concatenate([span_order, valid_frames]).astype(jnp.float16)
    meta_block = jnp.pad(meta[None, :], ((0, meta_rows - 1), (q_cols, kv_cols - 2 * slots)))
    weights_pair = lax.all_gather(jnp.concatenate([weights, meta_block], axis=0), "yh", axis=0)
    kv_gathered = lax.all_gather(
        weights_pair[:, :, q_cols:], ("z", "core"), axis=1, tiled=True
    ).reshape(-1, rows + meta_rows, kv_cols)
    kv_gathered, own_embed = lax.optimization_barrier((kv_gathered, own_embed))
    kv_full = kv_gathered[:, :rows].astype(jnp.bfloat16).reshape(-1, kv_cols)
    meta_all = jnp.sum(kv_gathered[:, rows:, : 2 * slots].astype(jnp.float32), axis=1)
    q_full = lax.all_gather(
        weights_pair[:, :rows, :q_cols].astype(jnp.bfloat16), ("z", "core"), axis=1, tiled=True
    ).reshape(-1, q_cols)

    other_embed = lax.ppermute(own_embed, "core", [(0, 1), (1, 0)])
    own_patches, other_patches = make_patches(scalars, clean_latents, noise, own_embed)
    normed_noisy, noisy_kv, clean_kv = embed_tokens(
        own_patches, other_patches, own_embed, other_embed, position, norm_gain, kv_full
    )

    clean_pair = lax.all_gather(clean_kv.astype(jnp.float16), "yh", axis=0)
    clean_all = lax.all_gather(clean_pair, ("z", "core"), axis=1, tiled=True)
    kv_all = clean_all.astype(jnp.bfloat16).reshape(-1, kv_cols)
    return attention(scalars, normed_noisy, q_full, noisy_kv, kv_all, meta_all)


def solution(mesh):
    fine = Mesh(mesh.devices.reshape(2, 16, 2, 4, 2), CTX + HEAD)
    return jax.shard_map(
        on_device,
        mesh=fine,
        in_specs=(
            P(CTX, None, None, None),
            P(CTX, None, None, None),
            P(CTX),
            P(CTX),
            P(CTX),
            P(None, HEAD),
            P(CTX, None),
            P(),
            P(CTX, HEAD),
            P(CTX, HEAD),
        ),
        out_specs=P(CTX, HEAD),
        check_vma=False,
    )
```

```python
import math

import jax
import jax.numpy as jnp
from jax import lax
from jax.experimental import pallas as pl
from jax.experimental.pallas import tpu as pltpu
from jax.sharding import Mesh, PartitionSpec as P

HD = 128
CH = 16


eps_norm = 1e-06
masked_low = -1e30


def in_hbm(array):
    return pltpu.with_memory_space_constraint(array, pltpu.HBM)


def patch_kernel(
    scalar_ref, clean_hbm, noise_hbm, after_ref, own_ref, other_ref, clean_ref, noise_ref, sems
):
    del after_ref
    loads = [
        pltpu.make_async_copy(clean_hbm, clean_ref, sems.at[0]),
        pltpu.make_async_copy(noise_hbm, noise_ref, sems.at[1]),
    ]
    for load in loads:
        load.start()
    rows, lanes = clean_ref.shape
    row = lax.broadcasted_iota(jnp.int32, (rows, lanes), 0)
    steps = jnp.where(row < rows // 2, scalar_ref[1], scalar_ref[2])
    level = (steps.astype(jnp.float32) + 1.0) / 1000.0
    for load in loads:
        load.wait()
    clean = clean_ref[...]
    noisy = (
        (1.0 - level) * clean.astype(jnp.float32) + level * noise_ref[...].astype(jnp.float32)
    ).astype(jnp.bfloat16)
    latents = jnp.concatenate([noisy, clean], axis=0)
    count = 2 * rows
    source = lax.broadcasted_iota(jnp.int32, (lanes, 256), 0)
    target = lax.broadcasted_iota(jnp.int32, (lanes, 256), 1)
    token = lax.broadcasted_iota(jnp.int32, (256, 4 * count), 0)
    place = lax.broadcasted_iota(jnp.int32, (256, 4 * count), 1)
    result = jnp.zeros((256, 256), jnp.float32)
    for kernel_row in range(4):
        shifted = []
        for token_col in range(4):
            wanted = (target & 63) + (32 * token_col - 16)
            pick = (source == wanted) & ((target >> 6) == kernel_row)
            pick = jnp.where(pick, 1.0, 0.0).astype(jnp.bfloat16)
            shifted.append(
                jnp.dot(latents, pick, preferred_element_type=jnp.float32).astype(jnp.bfloat16)
            )
        latent_row = 2 * ((token >> 2) & 3) - 1 + kernel_row
        wanted = (token & 3) * count + (token >> 4) * 8 + latent_row
        pick = (place == wanted) & (latent_row >= 0) & (latent_row < 8)
        pick = jnp.where(pick, 1.0, 0.0).astype(jnp.bfloat16)
        result += jnp.dot(pick, jnp.concatenate(shifted, axis=0), preferred_element_type=jnp.float32)
    patches = result.astype(jnp.bfloat16)
    half = patches.shape[1] // 2
    upper = scalar_ref[0] == 1
    own_ref[...] = jnp.where(upper, patches[:, half:], patches[:, :half])
    other_ref[...] = jnp.where(upper, patches[:, :half], patches[:, half:])


def make_patches(scalars, clean_latents, noise, after):
    flat = clean_latents.shape[-1]
    rows = clean_latents.size // flat
    hbm = pl.BlockSpec(memory_space=pltpu.HBM)
    vmem = pl.BlockSpec(memory_space=pltpu.VMEM)
    shape = jax.ShapeDtypeStruct((256, 128), jnp.bfloat16)
    return pl.pallas_call(
        patch_kernel,
        out_shape=(shape, shape),
        in_specs=[pl.BlockSpec(memory_space=pltpu.SMEM), hbm, hbm, hbm],
        out_specs=(vmem, vmem),
        scratch_shapes=[
            pltpu.VMEM((rows, flat), jnp.bfloat16),
            pltpu.VMEM((rows, flat), jnp.bfloat16),
            pltpu.SemaphoreType.DMA((2,)),
        ],
        compiler_params=pltpu.CompilerParams(vmem_limit_bytes=8 * 1024 * 1024),
    )(
        scalars,
        in_hbm(clean_latents.reshape(rows, flat)),
        in_hbm(noise.reshape(rows, flat)),
        in_hbm(after),
    )


CTX = ("yh", "z", "core")
HEAD = ("x", "yl")
meta_rows = 8
score_factor = HD ** (-0.5) * math.log2(math.e)
key_chunk = 1024
column_chunk = 768
embed_pieces = 4


def attention_kernel(
    scalar_ref, query_ref, own_ref, kv_hbm, meta_ref, out_ref, kv_ref, kv_sems
):
    orders = (scalar_ref[3], scalar_ref[4])
    valids = (scalar_ref[5], scalar_ref[6])
    tokens = query_ref.shape[0]
    group = query_ref.shape[1] // HD
    span_rows = tokens // 2
    frame_rows = span_rows // 4
    kv_copies = []
    chunk_blocks = key_chunk // tokens
    chunks = kv_ref.shape[0] // chunk_blocks
    for piece in range(chunks):
        part = pl.ds(piece * chunk_blocks, chunk_blocks)
        kv_copies.append(
            pltpu.make_async_copy(
                kv_hbm.at[part, pl.ds(0, tokens)], kv_ref.at[part], kv_sems.at[piece]
            )
        )
        kv_copies[-1].start()
    meta = meta_ref[...].astype(jnp.bfloat16)
    blocks = meta.shape[0]
    block_row = lax.broadcasted_iota(jnp.int32, (blocks, key_chunk), 0)
    block_col = lax.broadcasted_iota(jnp.int32, (blocks, key_chunk), 1)
    key_place = lax.broadcasted_iota(jnp.int32, (1, key_chunk), 1)
    second = (key_place & span_rows) != 0
    key_frame = ((key_place & (span_rows - 1)) // frame_rows).astype(jnp.float32)
    biases = []
    for piece in range(chunks):
        pick = block_row == ((block_col + piece * key_chunk) // tokens)
        spread = lax.dot_general(
            meta,
            jnp.where(pick, 1.0, 0.0).astype(jnp.bfloat16),
            (((0,), (0,)), ((), ())),
            preferred_element_type=jnp.float32,
        )
        key_order = jnp.where(second, spread[1:2], spread[0:1])
        key_valid = jnp.where(second, spread[3:4], spread[2:3])
        live = key_frame < key_valid
        biases.append(
            [
                jnp.where(live & (key_order < order.astype(jnp.float32)), 0.0, masked_low)
                for order in orders
            ]
        )
    queries = query_ref[...]
    q = jnp.concatenate([queries[:, g * HD : (g + 1) * HD] for g in range(group)], axis=0)

    def scores_of(keys, bias):
        s = lax.dot_general(q, keys, (((1,), (1,)), ((), ())), preferred_element_type=jnp.float32)
        s = s.reshape(group, tokens, keys.shape[0]) * score_factor + bias[None]
        return s.reshape(group * tokens, keys.shape[0])

    row = lax.broadcasted_iota(jnp.int32, (tokens, tokens), 0)
    col = lax.broadcasted_iota(jnp.int32, (tokens, tokens), 1)
    valid_col = jnp.where(col < span_rows, valids[0], valids[1])
    same = (row < span_rows) == (col < span_rows)
    live_col = lax.rem(col, span_rows) < valid_col * frame_rows
    own_bias = jnp.where(same & live_col, 0.0, masked_low)
    s = scores_of(own_ref[:, :HD], own_bias)
    largest = jnp.max(s, axis=1, keepdims=True)
    raw = jnp.exp2(s - largest)
    total = jnp.sum(raw, axis=1, keepdims=True)
    summed = jnp.dot(raw.astype(jnp.bfloat16), own_ref[:, HD:], preferred_element_type=jnp.float32)
    first = lax.broadcasted_iota(jnp.int32, (tokens, key_chunk), 0) < span_rows
    for piece in range(chunks):
        kv_copies[piece].wait()
        block = kv_ref[piece * chunk_blocks : (piece + 1) * chunk_blocks]
        block = block.reshape(key_chunk, 2 * HD)
        keys = block[:, :HD]
        values = block[:, HD:]
        bias = jnp.where(first, biases[piece][0], biases[piece][1])
        s = scores_of(keys, bias)
        new_largest = jnp.maximum(largest, jnp.max(s, axis=1, keepdims=True))
        raw = jnp.exp2(s - new_largest)
        factor = jnp.exp2(largest - new_largest)
        total = total * factor + jnp.sum(raw, axis=1, keepdims=True)
        summed = summed * factor + jnp.dot(
            raw.astype(jnp.bfloat16), values, preferred_element_type=jnp.float32
        )
        largest = new_largest
    result = summed / total
    token = lax.broadcasted_iota(jnp.int32, (tokens, HD), 0)
    valid_row = jnp.where(token < span_rows, valids[0], valids[1])
    live_row = lax.rem(token, span_rows) < valid_row * frame_rows
    for g in range(group):
        piece = result[g * tokens : (g + 1) * tokens]
        out_ref[:, g * HD : (g + 1) * HD] = jnp.where(live_row, piece, 0.0).astype(jnp.bfloat16)


def attention(scalars, queries, own, kv_all, meta):
    vmem = pl.BlockSpec(memory_space=pltpu.VMEM)
    hbm = pl.BlockSpec(memory_space=pltpu.HBM)
    tokens = queries.shape[0]
    blocks, unused, kv_cols = kv_all.shape
    return pl.pallas_call(
        attention_kernel,
        out_shape=jax.ShapeDtypeStruct(queries.shape, jnp.bfloat16),
        in_specs=[pl.BlockSpec(memory_space=pltpu.SMEM), vmem, vmem, hbm, vmem],
        out_specs=vmem,
        scratch_shapes=[
            pltpu.VMEM((blocks, tokens, kv_cols), jnp.bfloat16),
            pltpu.SemaphoreType.DMA((blocks * tokens // key_chunk,)),
        ],
        compiler_params=pltpu.CompilerParams(vmem_limit_bytes=28 * 1024 * 1024),
    )(scalars, queries, own, in_hbm(kv_all), meta)


def embed_kernel(
    own_patch_ref,
    other_patch_ref,
    own_embed_ref,
    other_embed_ref,
    position_ref,
    gain_ref,
    weight_ref,
    normed_ref,
    noisy_ref,
    clean_ref,
    embedded_ref,
    own_buffer,
    position_buffer,
    sems,
    out_sems,
):
    tokens, width = position_ref.shape
    piece_cols = width // embed_pieces
    copies = []
    for piece in range(embed_pieces):
        cols = pl.ds(piece * piece_cols, piece_cols)
        for index, (source, buffer) in enumerate(
            (
                (own_embed_ref, own_buffer),
                (position_ref, position_buffer),
            )
        ):
            copies.append(
                pltpu.make_async_copy(source.at[:, cols], buffer.at[:, cols], sems.at[index, piece])
            )
            copies[-1].start()
    patches = jnp.concatenate([own_patch_ref[...], other_patch_ref[...]], axis=1)
    squares = jnp.zeros((2 * tokens, 128), jnp.float32)
    for start in range(0, width, column_chunk):
        cols = slice(start, start + column_chunk)
        if start % piece_cols == 0:
            first = 2 * (start // piece_cols)
            for copy in copies[first : first + 2]:
                copy.wait()
        embed = jnp.concatenate([own_buffer[:, cols], other_embed_ref[:, cols]], axis=0)
        projected = jnp.dot(patches, embed, preferred_element_type=jnp.float32)
        place = position_buffer[:, cols].astype(jnp.float32)
        embedded = (projected + jnp.concatenate([place, place], axis=0)).astype(jnp.bfloat16)
        embedded_ref[:, cols] = embedded
        wide = embedded.astype(jnp.float32)
        for lane in range(0, column_chunk, 128):
            squares += wide[:, lane : lane + 128] * wide[:, lane : lane + 128]
    factor = lax.rsqrt(jnp.sum(squares, axis=1, keepdims=True) / width + eps_norm)
    summed = jnp.zeros((2 * tokens, weight_ref.shape[1]), jnp.float32)
    stores = []
    for start in range(0, width, column_chunk):
        cols = slice(start, start + column_chunk)
        wide = embedded_ref[:, cols].astype(jnp.float32)
        normed = (wide * factor * gain_ref[:, cols].astype(jnp.float32)).astype(jnp.bfloat16)
        embedded_ref[:tokens, cols] = normed[:tokens]
        if (start + column_chunk) % piece_cols == 0:
            piece = start // piece_cols
            done = pl.ds(piece * piece_cols, piece_cols)
            stores.append(
                pltpu.make_async_copy(
                    embedded_ref.at[:tokens, done], normed_ref.at[:, done], out_sems.at[piece]
                )
            )
            stores[-1].start()
        summed += jnp.dot(normed, weight_ref[cols, :], preferred_element_type=jnp.float32)
    noisy_ref[...] = summed[:tokens].astype(jnp.bfloat16)
    clean_ref[...] = summed[tokens:].astype(jnp.bfloat16)
    for store in stores:
        store.wait()


def embed_tokens(own_patches, other_patches, own_embed, other_embed, position, gain, weight):
    tokens, width = position.shape
    vmem = pl.BlockSpec(memory_space=pltpu.VMEM)
    hbm = pl.BlockSpec(memory_space=pltpu.HBM)
    kv_shape = jax.ShapeDtypeStruct((tokens, weight.shape[1]), jnp.bfloat16)
    return pl.pallas_call(
        embed_kernel,
        out_shape=(pltpu.HBM((tokens, width), jnp.bfloat16), kv_shape, kv_shape),
        in_specs=[vmem, vmem, hbm, vmem, hbm, vmem, vmem],
        out_specs=(hbm, vmem, vmem),
        scratch_shapes=[
            pltpu.VMEM((2 * tokens, width), jnp.bfloat16),
            pltpu.VMEM(own_embed.shape, jnp.bfloat16),
            pltpu.VMEM(position.shape, jnp.bfloat16),
            pltpu.SemaphoreType.DMA((2, embed_pieces)),
            pltpu.SemaphoreType.DMA((embed_pieces,)),
        ],
        compiler_params=pltpu.CompilerParams(vmem_limit_bytes=24 * 1024 * 1024),
    )(
        own_patches,
        other_patches,
        in_hbm(own_embed),
        other_embed,
        in_hbm(position),
        gain[None],
        weight,
    )


def on_device(
    clean_latents,
    noise,
    timesteps,
    span_order,
    valid_frames,
    embed_weight,
    position,
    norm_gain,
    query_weight,
    kv_weight,
):
    slots = clean_latents.shape[0]
    core = lax.axis_index("core")
    half = embed_weight.shape[0] // 2
    scalars = in_hbm(jnp.concatenate([core[None], timesteps, span_order, valid_frames]))
    own_embed = lax.all_gather(
        lax.dynamic_slice_in_dim(embed_weight, core * half, half, 0), HEAD, axis=1, tiled=True
    )
    kv_cols = kv_weight.shape[1]
    q_cols = query_weight.shape[1]
    weights = jnp.concatenate([query_weight, kv_weight], axis=1).astype(jnp.float16)
    weights_pair = lax.all_gather(weights, "yh", axis=0)
    gathered = lax.all_gather(weights_pair, ("z", "core"), axis=1, tiled=True)
    gathered, own_embed = lax.optimization_barrier((gathered, own_embed))
    gathered = gathered.reshape(-1, q_cols + kv_cols)
    kv_full = gathered[:, q_cols:].astype(jnp.bfloat16)

    other_embed = lax.ppermute(own_embed, "core", [(0, 1), (1, 0)])
    own_patches, other_patches = make_patches(scalars, clean_latents, noise, own_embed)
    normed_noisy, noisy_kv, clean_kv = embed_tokens(
        own_patches, other_patches, own_embed, other_embed, position, norm_gain, kv_full
    )

    queries = jnp.dot(
        normed_noisy,
        gathered[:, :q_cols].astype(jnp.bfloat16),
        preferred_element_type=jnp.float32,
    ).astype(jnp.bfloat16)

    tokens = clean_kv.shape[0]
    meta = jnp.concatenate([span_order, valid_frames]).astype(jnp.float16)
    meta_block = jnp.pad(meta[None, :], ((0, meta_rows - 1), (0, kv_cols - 2 * slots)))
    clean = jnp.concatenate([clean_kv.astype(jnp.float16), meta_block], axis=0)
    clean_pair = lax.all_gather(clean, "yh", axis=0)
    clean_all = lax.all_gather(clean_pair, ("z", "core"), axis=1, tiled=True)
    clean_all = clean_all.reshape(-1, tokens + meta_rows, kv_cols)
    meta_all = jnp.sum(clean_all[:, tokens:, : 2 * slots].astype(jnp.float32), axis=1)
    return attention(scalars, queries, noisy_kv, clean_all.astype(jnp.bfloat16), meta_all)


def solution(mesh):
    fine = Mesh(mesh.devices.reshape(2, 16, 2, 4, 2), CTX + HEAD)
    return jax.shard_map(
        on_device,
        mesh=fine,
        in_specs=(
            P(CTX, None, None, None),
            P(CTX, None, None, None),
            P(CTX),
            P(CTX),
            P(CTX),
            P(None, HEAD),
            P(CTX, None),
            P(),
            P(CTX, HEAD),
            P(CTX, HEAD),
        ),
        out_specs=P(CTX, HEAD),
        check_vma=False,
    )
```

```python
import math

import jax
import jax.numpy as jnp
from jax import lax
from jax.experimental import pallas as pl
from jax.experimental.pallas import tpu as pltpu
from jax.sharding import Mesh, PartitionSpec as P

HD = 128
CH = 16


eps_norm = 1e-06
masked_low = -1e30


def in_hbm(array):
    return pltpu.with_memory_space_constraint(array, pltpu.HBM)


def patch_kernel(
    time_ref, clean_hbm, noise_hbm, after_ref, own_ref, other_ref, clean_ref, noise_ref, sems
):
    del after_ref
    loads = [
        pltpu.make_async_copy(clean_hbm, clean_ref, sems.at[0]),
        pltpu.make_async_copy(noise_hbm, noise_ref, sems.at[1]),
    ]
    for load in loads:
        load.start()
    rows, lanes = clean_ref.shape
    row = lax.broadcasted_iota(jnp.int32, (rows, lanes), 0)
    steps = jnp.where(row < rows // 2, time_ref[0], time_ref[1])
    level = (steps.astype(jnp.float32) + 1.0) / 1000.0
    for load in loads:
        load.wait()
    clean = clean_ref[...]
    noisy = (
        (1.0 - level) * clean.astype(jnp.float32) + level * noise_ref[...].astype(jnp.float32)
    ).astype(jnp.bfloat16)
    latents = jnp.concatenate([noisy, clean], axis=0)
    count = 2 * rows
    source = lax.broadcasted_iota(jnp.int32, (lanes, 256), 0)
    target = lax.broadcasted_iota(jnp.int32, (lanes, 256), 1)
    token = lax.broadcasted_iota(jnp.int32, (256, 4 * count), 0)
    place = lax.broadcasted_iota(jnp.int32, (256, 4 * count), 1)
    result = jnp.zeros((256, 256), jnp.float32)
    for kernel_row in range(4):
        shifted = []
        for token_col in range(4):
            wanted = (target & 63) + (32 * token_col - 16)
            pick = (source == wanted) & ((target >> 6) == kernel_row)
            pick = jnp.where(pick, 1.0, 0.0).astype(jnp.bfloat16)
            shifted.append(
                jnp.dot(latents, pick, preferred_element_type=jnp.float32).astype(jnp.bfloat16)
            )
        latent_row = 2 * ((token >> 2) & 3) - 1 + kernel_row
        wanted = (token & 3) * count + (token >> 4) * 8 + latent_row
        pick = (place == wanted) & (latent_row >= 0) & (latent_row < 8)
        pick = jnp.where(pick, 1.0, 0.0).astype(jnp.bfloat16)
        result += jnp.dot(pick, jnp.concatenate(shifted, axis=0), preferred_element_type=jnp.float32)
    patches = result.astype(jnp.bfloat16)
    half = patches.shape[1] // 2
    upper = lax.axis_index("core") == 1
    own_ref[...] = jnp.where(upper, patches[:, half:], patches[:, :half])
    other_ref[...] = jnp.where(upper, patches[:, :half], patches[:, half:])


def make_patches(timesteps, clean_latents, noise, after):
    flat = clean_latents.shape[-1]
    rows = clean_latents.size // flat
    hbm = pl.BlockSpec(memory_space=pltpu.HBM)
    vmem = pl.BlockSpec(memory_space=pltpu.VMEM)
    shape = jax.ShapeDtypeStruct((256, 128), jnp.bfloat16)
    return pl.pallas_call(
        patch_kernel,
        out_shape=(shape, shape),
        in_specs=[pl.BlockSpec(memory_space=pltpu.SMEM), hbm, hbm, hbm],
        out_specs=(vmem, vmem),
        scratch_shapes=[
            pltpu.VMEM((rows, flat), jnp.bfloat16),
            pltpu.VMEM((rows, flat), jnp.bfloat16),
            pltpu.SemaphoreType.DMA((2,)),
        ],
        compiler_params=pltpu.CompilerParams(vmem_limit_bytes=8 * 1024 * 1024),
    )(
        in_hbm(timesteps),
        in_hbm(clean_latents.reshape(rows, flat)),
        in_hbm(noise.reshape(rows, flat)),
        in_hbm(after),
    )


CTX = ("yh", "z", "core")
HEAD = ("x", "yl")
meta_rows = 8
score_factor = HD ** (-0.5) * math.log2(math.e)
key_chunk = 1024
column_chunk = 768
embed_pieces = 4


def attention_kernel(
    order_ref, valid_ref, query_ref, own_ref, kv_hbm, meta_ref, out_ref, kv_ref, kv_sems
):
    tokens = query_ref.shape[0]
    group = query_ref.shape[1] // HD
    span_rows = tokens // 2
    frame_rows = span_rows // 4
    chunk_blocks = key_chunk // span_rows
    chunks = kv_ref.shape[0] // chunk_blocks
    kv_copies = []
    for piece in range(chunks):
        part = pl.ds(piece * chunk_blocks, chunk_blocks)
        kv_copies.append(
            pltpu.make_async_copy(
                kv_hbm.at[part, pl.ds(0, tokens)], kv_ref.at[part], kv_sems.at[piece]
            )
        )
        kv_copies[-1].start()
    swap, orders, valids = ordered_spans(order_ref, valid_ref)
    queries = swap_spans(query_ref[...], swap)
    own = swap_spans(own_ref[...], swap)
    q = jnp.concatenate(
        [
            queries[slot * span_rows : (slot + 1) * span_rows, g * HD : (g + 1) * HD]
            for slot in range(2)
            for g in range(group)
        ],
        axis=0,
    )
    slot_rows = group * span_rows

    def scores_of(rows, keys):
        return lax.dot_general(
            rows, keys, (((1,), (1,)), ((), ())), preferred_element_type=jnp.float32
        )

    col = lax.broadcasted_iota(jnp.int32, (1, tokens), 1)
    states = []
    for slot in range(2):
        inside = (col >= slot * span_rows) & (
            col < slot * span_rows + valids[slot] * frame_rows
        )
        s = scores_of(q[slot * slot_rows : (slot + 1) * slot_rows], own[:, :HD]) * score_factor
        s += jnp.where(inside, 0.0, masked_low)
        largest = jnp.max(s, axis=1, keepdims=True)
        raw = jnp.exp2(s - largest)
        total = jnp.sum(raw, axis=1, keepdims=True)
        summed = jnp.dot(
            raw.astype(jnp.bfloat16), own[:, HD:], preferred_element_type=jnp.float32
        )
        states.append((largest, total, summed))

    def fold(state, s, values):
        largest, total, summed = state
        new_largest = jnp.maximum(largest, jnp.max(s, axis=1, keepdims=True))
        raw = jnp.exp2(s - new_largest)
        factor = jnp.exp2(largest - new_largest)
        total = total * factor + jnp.sum(raw, axis=1, keepdims=True)
        summed = summed * factor + jnp.dot(
            raw.astype(jnp.bfloat16), values, preferred_element_type=jnp.float32
        )
        return (new_largest, total, summed)

    block_row = lax.broadcasted_iota(jnp.int32, (chunk_blocks, key_chunk), 0)
    block_col = lax.broadcasted_iota(jnp.int32, (chunk_blocks, key_chunk), 1)
    pick = jnp.where(block_row == block_col // span_rows, 1.0, 0.0).astype(jnp.bfloat16)
    key_place = lax.broadcasted_iota(jnp.int32, (1, key_chunk), 1)
    key_frame = ((key_place & (span_rows - 1)) // frame_rows).astype(jnp.float32)
    limits = [order.astype(jnp.float32) for order in orders]
    for piece in range(chunks):
        part = slice(piece * chunk_blocks, (piece + 1) * chunk_blocks)
        spread = lax.dot_general(
            meta_ref[part, :].astype(jnp.bfloat16),
            pick,
            (((0,), (0,)), ((), ())),
            preferred_element_type=jnp.float32,
        )
        kv_copies[piece].wait()
        for key_slot in range(2):
            block = kv_ref[part, key_slot * span_rows : (key_slot + 1) * span_rows, :]
            block = block.reshape(key_chunk, 2 * HD)
            key_order = spread[key_slot : key_slot + 1]
            live = key_frame < spread[2 + key_slot : 3 + key_slot]
            s = scores_of(q[key_slot * slot_rows :], block[:, :HD]) * score_factor
            for slot in range(key_slot, 2):
                bias = jnp.where(live & (key_order < limits[slot]), 0.0, masked_low)
                begin = (slot - key_slot) * slot_rows
                states[slot] = fold(
                    states[slot], s[begin : begin + slot_rows] + bias, block[:, HD:]
                )

    token = lax.broadcasted_iota(jnp.int32, (span_rows, HD), 0)
    pieces = []
    for slot in range(2):
        largest, total, summed = states[slot]
        result = summed / total
        live_row = token < valids[slot] * frame_rows
        pieces.append(
            jnp.concatenate(
                [
                    jnp.where(live_row, result[g * span_rows : (g + 1) * span_rows], 0.0)
                    for g in range(group)
                ],
                axis=1,
            )
        )
    out_ref[...] = swap_spans(jnp.concatenate(pieces, axis=0), swap).astype(jnp.bfloat16)


def attention(order, valid, queries, own, kv_all, meta):
    smem = pl.BlockSpec(memory_space=pltpu.SMEM)
    vmem = pl.BlockSpec(memory_space=pltpu.VMEM)
    hbm = pl.BlockSpec(memory_space=pltpu.HBM)
    tokens = queries.shape[0]
    blocks, unused, kv_cols = kv_all.shape
    return pl.pallas_call(
        attention_kernel,
        out_shape=jax.ShapeDtypeStruct(queries.shape, jnp.bfloat16),
        in_specs=[smem, smem, vmem, vmem, hbm, vmem],
        out_specs=vmem,
        scratch_shapes=[
            pltpu.VMEM((blocks, tokens, kv_cols), jnp.bfloat16),
            pltpu.SemaphoreType.DMA((blocks * tokens // (2 * key_chunk),)),
        ],
        compiler_params=pltpu.CompilerParams(vmem_limit_bytes=28 * 1024 * 1024),
    )(in_hbm(order), in_hbm(valid), queries, own, in_hbm(kv_all), meta)


def ordered_spans(order_ref, valid_ref):
    swap = order_ref[0] > order_ref[1]
    orders = (jnp.minimum(order_ref[0], order_ref[1]), jnp.maximum(order_ref[0], order_ref[1]))
    valids = (
        jnp.where(swap, valid_ref[1], valid_ref[0]),
        jnp.where(swap, valid_ref[0], valid_ref[1]),
    )
    return swap, orders, valids


def swap_spans(values, swap):
    rows = values.shape[0] // 2
    turned = jnp.concatenate([values[rows:], values[:rows]], axis=0)
    return jnp.where(swap, turned, values)


def embed_kernel(
    order_ref,
    valid_ref,
    own_patch_ref,
    other_patch_ref,
    own_embed_ref,
    other_embed_ref,
    position_ref,
    gain_ref,
    weight_ref,
    normed_ref,
    noisy_ref,
    clean_ref,
    embedded_ref,
    own_buffer,
    position_buffer,
    sems,
    out_sems,
):
    tokens, width = position_ref.shape
    piece_cols = width // embed_pieces
    copies = []
    for piece in range(embed_pieces):
        cols = pl.ds(piece * piece_cols, piece_cols)
        for index, (source, buffer) in enumerate(
            (
                (own_embed_ref, own_buffer),
                (position_ref, position_buffer),
            )
        ):
            copies.append(
                pltpu.make_async_copy(source.at[:, cols], buffer.at[:, cols], sems.at[index, piece])
            )
            copies[-1].start()
    patches = jnp.concatenate([own_patch_ref[...], other_patch_ref[...]], axis=1)
    squares = jnp.zeros((2 * tokens, 128), jnp.float32)
    for start in range(0, width, column_chunk):
        cols = slice(start, start + column_chunk)
        if start % piece_cols == 0:
            first = 2 * (start // piece_cols)
            for copy in copies[first : first + 2]:
                copy.wait()
        embed = jnp.concatenate([own_buffer[:, cols], other_embed_ref[:, cols]], axis=0)
        projected = jnp.dot(patches, embed, preferred_element_type=jnp.float32)
        place = position_buffer[:, cols].astype(jnp.float32)
        embedded = (projected + jnp.concatenate([place, place], axis=0)).astype(jnp.bfloat16)
        embedded_ref[:, cols] = embedded
        wide = embedded.astype(jnp.float32)
        for lane in range(0, column_chunk, 128):
            squares += wide[:, lane : lane + 128] * wide[:, lane : lane + 128]
    factor = lax.rsqrt(jnp.sum(squares, axis=1, keepdims=True) / width + eps_norm)
    summed = jnp.zeros((2 * tokens, weight_ref.shape[1]), jnp.float32)
    stores = []
    for start in range(0, width, column_chunk):
        cols = slice(start, start + column_chunk)
        wide = embedded_ref[:, cols].astype(jnp.float32)
        gain = jnp.concatenate(
            [
                gain_ref[row : row + 1, :]
                for row in range(start // 128, (start + column_chunk) // 128)
            ],
            axis=1,
        )
        normed = (wide * factor * gain.astype(jnp.float32)).astype(jnp.bfloat16)
        embedded_ref[:tokens, cols] = normed[:tokens]
        if (start + column_chunk) % piece_cols == 0:
            piece = start // piece_cols
            done = pl.ds(piece * piece_cols, piece_cols)
            stores.append(
                pltpu.make_async_copy(
                    embedded_ref.at[:tokens, done], normed_ref.at[:, done], out_sems.at[piece]
                )
            )
            stores[-1].start()
        summed += jnp.dot(normed, weight_ref[cols, :], preferred_element_type=jnp.float32)
    noisy_ref[...] = summed[:tokens].astype(jnp.bfloat16)
    swap, orders, valids = ordered_spans(order_ref, valid_ref)
    clean_ref[:tokens, :] = swap_spans(summed[tokens:], swap).astype(jnp.bfloat16)
    lane = lax.broadcasted_iota(jnp.int32, (meta_rows, summed.shape[1]), 1)
    first_row = lax.broadcasted_iota(jnp.int32, lane.shape, 0) == 0
    table = jnp.zeros(lane.shape, jnp.float32)
    for place, entry in enumerate(orders + valids):
        table = jnp.where(first_row & (lane == place), entry.astype(jnp.float32), table)
    clean_ref[tokens:, :] = table.astype(jnp.bfloat16)
    for store in stores:
        store.wait()


def embed_tokens(
    order, valid, own_patches, other_patches, own_embed, other_embed, position, gain, weight
):
    tokens, width = position.shape
    vmem = pl.BlockSpec(memory_space=pltpu.VMEM)
    hbm = pl.BlockSpec(memory_space=pltpu.HBM)
    smem = pl.BlockSpec(memory_space=pltpu.SMEM)
    kv_shape = jax.ShapeDtypeStruct((tokens, weight.shape[1]), jnp.bfloat16)
    clean_shape = jax.ShapeDtypeStruct((tokens + meta_rows, weight.shape[1]), jnp.bfloat16)
    return pl.pallas_call(
        embed_kernel,
        out_shape=(pltpu.HBM((tokens, width), jnp.bfloat16), kv_shape, clean_shape),
        in_specs=[smem, smem, vmem, vmem, hbm, vmem, hbm, vmem, vmem],
        out_specs=(hbm, vmem, vmem),
        scratch_shapes=[
            pltpu.VMEM((2 * tokens, width), jnp.bfloat16),
            pltpu.VMEM(own_embed.shape, jnp.bfloat16),
            pltpu.VMEM(position.shape, jnp.bfloat16),
            pltpu.SemaphoreType.DMA((2, embed_pieces)),
            pltpu.SemaphoreType.DMA((embed_pieces,)),
        ],
        compiler_params=pltpu.CompilerParams(vmem_limit_bytes=24 * 1024 * 1024),
    )(
        in_hbm(order),
        in_hbm(valid),
        own_patches,
        other_patches,
        in_hbm(own_embed),
        other_embed,
        in_hbm(position),
        gain.reshape(-1, 128),
        weight,
    )


def on_device(
    clean_latents,
    noise,
    timesteps,
    span_order,
    valid_frames,
    embed_weight,
    position,
    norm_gain,
    query_weight,
    kv_weight,
):
    core = lax.axis_index("core")
    half = embed_weight.shape[0] // 2
    own_embed = lax.all_gather(
        lax.dynamic_slice_in_dim(embed_weight, core * half, half, 0), HEAD, axis=1, tiled=True
    )
    kv_cols = kv_weight.shape[1]
    q_cols = query_weight.shape[1]
    weights = jnp.concatenate([query_weight, kv_weight], axis=1).astype(jnp.float16)
    weights_pair = lax.all_gather(weights, "yh", axis=0)
    gathered = lax.all_gather(weights_pair, ("z", "core"), axis=1, tiled=True)
    gathered, own_embed = lax.optimization_barrier((gathered, own_embed))
    gathered = gathered.reshape(-1, q_cols + kv_cols)
    kv_full = gathered[:, q_cols:].astype(jnp.bfloat16)

    other_embed = lax.ppermute(own_embed, "core", [(0, 1), (1, 0)])
    own_patches, other_patches = make_patches(timesteps, clean_latents, noise, own_embed)
    normed_noisy, noisy_kv, clean_kv = embed_tokens(
        span_order,
        valid_frames,
        own_patches,
        other_patches,
        own_embed,
        other_embed,
        position,
        norm_gain,
        kv_full,
    )

    queries = jnp.dot(
        normed_noisy,
        gathered[:, :q_cols].astype(jnp.bfloat16),
        preferred_element_type=jnp.float32,
    ).astype(jnp.bfloat16)

    slots = span_order.shape[0]
    rows = clean_kv.shape[0]
    clean_pair = lax.all_gather(clean_kv.astype(jnp.float16), "yh", axis=0)
    clean_all = lax.all_gather(clean_pair, ("z", "core"), axis=1, tiled=True)
    clean_all = clean_all.reshape(-1, rows, kv_cols)
    meta_all = jnp.sum(clean_all[:, rows - meta_rows :, : 2 * slots].astype(jnp.float32), axis=1)
    return attention(
        span_order, valid_frames, queries, noisy_kv, clean_all.astype(jnp.bfloat16), meta_all
    )


def solution(mesh):
    fine = Mesh(mesh.devices.reshape(2, 16, 2, 4, 2), CTX + HEAD)
    return jax.shard_map(
        on_device,
        mesh=fine,
        in_specs=(
            P(CTX, None, None, None),
            P(CTX, None, None, None),
            P(CTX),
            P(CTX),
            P(CTX),
            P(None, HEAD),
            P(CTX, None),
            P(),
            P(CTX, HEAD),
            P(CTX, HEAD),
        ),
        out_specs=P(CTX, HEAD),
        check_vma=False,
    )
```

```python
import math

import jax
import jax.numpy as jnp
from jax import lax
from jax.experimental import pallas as pl
from jax.experimental.pallas import tpu as pltpu
from jax.sharding import Mesh, PartitionSpec as P

HD = 128
CH = 16


eps_norm = 1e-06
masked_low = -1e30


def in_hbm(array):
    return pltpu.with_memory_space_constraint(array, pltpu.HBM)


def ordered_spans(order_ref, valid_ref):
    swap = order_ref[0] > order_ref[1]
    orders = (jnp.minimum(order_ref[0], order_ref[1]), jnp.maximum(order_ref[0], order_ref[1]))
    valids = (
        jnp.where(swap, valid_ref[1], valid_ref[0]),
        jnp.where(swap, valid_ref[0], valid_ref[1]),
    )
    return swap, orders, valids


def swap_spans(values, swap):
    rows = values.shape[0] // 2
    turned = jnp.concatenate([values[rows:], values[:rows]], axis=0)
    return jnp.where(swap, turned, values)


def patch_kernel(
    time_ref,
    order_ref,
    valid_ref,
    clean_hbm,
    noise_hbm,
    after_ref,
    own_ref,
    other_ref,
    plan_ref,
    clean_ref,
    noise_ref,
    sems,
):
    del after_ref
    loads = [
        pltpu.make_async_copy(clean_hbm, clean_ref, sems.at[0]),
        pltpu.make_async_copy(noise_hbm, noise_ref, sems.at[1]),
    ]
    for load in loads:
        load.start()
    rows, lanes = clean_ref.shape
    row = lax.broadcasted_iota(jnp.int32, (rows, lanes), 0)
    steps = jnp.where(row < rows // 2, time_ref[0], time_ref[1])
    level = (steps.astype(jnp.float32) + 1.0) / 1000.0
    for load in loads:
        load.wait()
    clean = clean_ref[...]
    noisy = (
        (1.0 - level) * clean.astype(jnp.float32) + level * noise_ref[...].astype(jnp.float32)
    ).astype(jnp.bfloat16)
    latents = jnp.concatenate([noisy, clean], axis=0)
    count = 2 * rows
    source = lax.broadcasted_iota(jnp.int32, (lanes, 256), 0)
    target = lax.broadcasted_iota(jnp.int32, (lanes, 256), 1)
    token = lax.broadcasted_iota(jnp.int32, (256, 4 * count), 0)
    place = lax.broadcasted_iota(jnp.int32, (256, 4 * count), 1)
    result = jnp.zeros((256, 256), jnp.float32)
    for kernel_row in range(4):
        shifted = []
        for token_col in range(4):
            wanted = (target & 63) + (32 * token_col - 16)
            pick = (source == wanted) & ((target >> 6) == kernel_row)
            pick = jnp.where(pick, 1.0, 0.0).astype(jnp.bfloat16)
            shifted.append(
                jnp.dot(latents, pick, preferred_element_type=jnp.float32).astype(jnp.bfloat16)
            )
        latent_row = 2 * ((token >> 2) & 3) - 1 + kernel_row
        wanted = (token & 3) * count + (token >> 4) * 8 + latent_row
        pick = (place == wanted) & (latent_row >= 0) & (latent_row < 8)
        pick = jnp.where(pick, 1.0, 0.0).astype(jnp.bfloat16)
        result += jnp.dot(pick, jnp.concatenate(shifted, axis=0), preferred_element_type=jnp.float32)
    patches = result.astype(jnp.bfloat16)
    half = patches.shape[1] // 2
    upper = lax.axis_index("core") == 1
    own_ref[...] = jnp.where(upper, patches[:, half:], patches[:, :half])
    other_ref[...] = jnp.where(upper, patches[:, :half], patches[:, half:])
    swap, orders, valids = ordered_spans(order_ref, valid_ref)
    lane = lax.broadcasted_iota(jnp.int32, plan_ref.shape, 1)
    plan_row = lax.broadcasted_iota(jnp.int32, plan_ref.shape, 0)
    plan = jnp.where(plan_row == 1, jnp.where(swap, 1.0, 0.0), 0.0)
    for place, entry in enumerate(orders + valids):
        plan = jnp.where((plan_row == 0) & (lane == place), entry.astype(jnp.float32), plan)
    plan_ref[...] = plan


def make_patches(timesteps, order, valid, clean_latents, noise, after):
    smem = pl.BlockSpec(memory_space=pltpu.SMEM)
    flat = clean_latents.shape[-1]
    rows = clean_latents.size // flat
    hbm = pl.BlockSpec(memory_space=pltpu.HBM)
    vmem = pl.BlockSpec(memory_space=pltpu.VMEM)
    shape = jax.ShapeDtypeStruct((256, 128), jnp.bfloat16)
    return pl.pallas_call(
        patch_kernel,
        out_shape=(shape, shape, jax.ShapeDtypeStruct((meta_rows, 256), jnp.float32)),
        in_specs=[smem, smem, smem, hbm, hbm, hbm],
        out_specs=(vmem, vmem, vmem),
        scratch_shapes=[
            pltpu.VMEM((rows, flat), jnp.bfloat16),
            pltpu.VMEM((rows, flat), jnp.bfloat16),
            pltpu.SemaphoreType.DMA((2,)),
        ],
        compiler_params=pltpu.CompilerParams(vmem_limit_bytes=8 * 1024 * 1024),
    )(
        in_hbm(timesteps),
        in_hbm(order),
        in_hbm(valid),
        in_hbm(clean_latents.reshape(rows, flat)),
        in_hbm(noise.reshape(rows, flat)),
        in_hbm(after),
    )


CTX = ("yh", "z", "core")
HEAD = ("x", "yl")
meta_rows = 8
score_factor = HD ** (-0.5) * math.log2(math.e)
key_chunk = 1024
column_chunk = 768
embed_pieces = 4


def attention_kernel(
    order_ref, valid_ref, query_ref, own_ref, kv_ref, meta_ref, out_ref
):
    tokens = query_ref.shape[0]
    group = query_ref.shape[1] // HD
    span_rows = tokens // 2
    frame_rows = span_rows // 4
    chunk_blocks = key_chunk // span_rows
    chunks = kv_ref.shape[0] // chunk_blocks
    swap, orders, valids = ordered_spans(order_ref, valid_ref)
    queries = swap_spans(query_ref[...], swap)
    own = swap_spans(own_ref[...], swap)
    q = jnp.concatenate(
        [
            queries[slot * span_rows : (slot + 1) * span_rows, g * HD : (g + 1) * HD]
            for slot in range(2)
            for g in range(group)
        ],
        axis=0,
    )
    slot_rows = group * span_rows

    def scores_of(rows, keys):
        return lax.dot_general(
            rows, keys, (((1,), (1,)), ((), ())), preferred_element_type=jnp.float32
        )

    col = lax.broadcasted_iota(jnp.int32, (1, tokens), 1)
    states = []
    for slot in range(2):
        inside = (col >= slot * span_rows) & (
            col < slot * span_rows + valids[slot] * frame_rows
        )
        s = scores_of(q[slot * slot_rows : (slot + 1) * slot_rows], own[:, :HD]) * score_factor
        s += jnp.where(inside, 0.0, masked_low)
        largest = jnp.max(s, axis=1, keepdims=True)
        raw = jnp.exp2(s - largest)
        total = jnp.sum(raw, axis=1, keepdims=True)
        summed = jnp.dot(
            raw.astype(jnp.bfloat16), own[:, HD:], preferred_element_type=jnp.float32
        )
        states.append((largest, total, summed))

    def fold(state, s, values):
        largest, total, summed = state
        new_largest = jnp.maximum(largest, jnp.max(s, axis=1, keepdims=True))
        raw = jnp.exp2(s - new_largest)
        factor = jnp.exp2(largest - new_largest)
        total = total * factor + jnp.sum(raw, axis=1, keepdims=True)
        summed = summed * factor + jnp.dot(
            raw.astype(jnp.bfloat16), values, preferred_element_type=jnp.float32
        )
        return (new_largest, total, summed)

    block_row = lax.broadcasted_iota(jnp.int32, (chunk_blocks, key_chunk), 0)
    block_col = lax.broadcasted_iota(jnp.int32, (chunk_blocks, key_chunk), 1)
    pick = jnp.where(block_row == block_col // span_rows, 1.0, 0.0).astype(jnp.bfloat16)
    key_place = lax.broadcasted_iota(jnp.int32, (1, key_chunk), 1)
    key_frame = ((key_place & (span_rows - 1)) // frame_rows).astype(jnp.float32)
    limits = [order.astype(jnp.float32) for order in orders]
    for piece in range(chunks):
        part = slice(piece * chunk_blocks, (piece + 1) * chunk_blocks)
        spread = lax.dot_general(
            meta_ref[part, :].astype(jnp.bfloat16),
            pick,
            (((0,), (0,)), ((), ())),
            preferred_element_type=jnp.float32,
        )
        for key_slot in range(2):
            block = kv_ref[part, key_slot * span_rows : (key_slot + 1) * span_rows, :]
            block = block.reshape(key_chunk, 2 * HD)
            key_order = spread[key_slot : key_slot + 1]
            live = key_frame < spread[2 + key_slot : 3 + key_slot]
            s = scores_of(q[key_slot * slot_rows :], block[:, :HD]) * score_factor
            for slot in range(key_slot, 2):
                bias = jnp.where(live & (key_order < limits[slot]), 0.0, masked_low)
                begin = (slot - key_slot) * slot_rows
                states[slot] = fold(
                    states[slot], s[begin : begin + slot_rows] + bias, block[:, HD:]
                )

    token = lax.broadcasted_iota(jnp.int32, (span_rows, HD), 0)
    pieces = []
    for slot in range(2):
        largest, total, summed = states[slot]
        result = summed / total
        live_row = token < valids[slot] * frame_rows
        pieces.append(
            jnp.concatenate(
                [
                    jnp.where(live_row, result[g * span_rows : (g + 1) * span_rows], 0.0)
                    for g in range(group)
                ],
                axis=1,
            )
        )
    out_ref[...] = swap_spans(jnp.concatenate(pieces, axis=0), swap).astype(jnp.bfloat16)


def attention(order, valid, queries, own, kv_all, meta):
    smem = pl.BlockSpec(memory_space=pltpu.SMEM)
    vmem = pl.BlockSpec(memory_space=pltpu.VMEM)
    return pl.pallas_call(
        attention_kernel,
        out_shape=jax.ShapeDtypeStruct(queries.shape, jnp.bfloat16),
        in_specs=[smem, smem, vmem, vmem, vmem, vmem],
        out_specs=vmem,
        compiler_params=pltpu.CompilerParams(vmem_limit_bytes=16 * 1024 * 1024),
    )(in_hbm(order), in_hbm(valid), queries, own, kv_all, meta)


def embed_kernel(
    plan_ref,
    own_patch_ref,
    other_patch_ref,
    own_embed_ref,
    other_embed_ref,
    position_ref,
    gain_ref,
    weight_ref,
    normed_ref,
    noisy_ref,
    clean_ref,
    embedded_ref,
    own_buffer,
    position_buffer,
    sems,
    out_sems,
):
    tokens, width = position_ref.shape
    piece_cols = width // embed_pieces
    copies = []
    for piece in range(embed_pieces):
        cols = pl.ds(piece * piece_cols, piece_cols)
        for index, (source, buffer) in enumerate(
            (
                (own_embed_ref, own_buffer),
                (position_ref, position_buffer),
            )
        ):
            copies.append(
                pltpu.make_async_copy(source.at[:, cols], buffer.at[:, cols], sems.at[index, piece])
            )
            copies[-1].start()
    patches = jnp.concatenate([own_patch_ref[...], other_patch_ref[...]], axis=1)
    squares = jnp.zeros((2 * tokens, 128), jnp.float32)
    for start in range(0, width, column_chunk):
        cols = slice(start, start + column_chunk)
        if start % piece_cols == 0:
            first = 2 * (start // piece_cols)
            for copy in copies[first : first + 2]:
                copy.wait()
        embed = jnp.concatenate([own_buffer[:, cols], other_embed_ref[:, cols]], axis=0)
        projected = jnp.dot(patches, embed, preferred_element_type=jnp.float32)
        place = position_buffer[:, cols].astype(jnp.float32)
        embedded = (projected + jnp.concatenate([place, place], axis=0)).astype(jnp.bfloat16)
        embedded_ref[:, cols] = embedded
        wide = embedded.astype(jnp.float32)
        for lane in range(0, column_chunk, 128):
            squares += wide[:, lane : lane + 128] * wide[:, lane : lane + 128]
    factor = lax.rsqrt(jnp.sum(squares, axis=1, keepdims=True) / width + eps_norm)
    summed = jnp.zeros((2 * tokens, weight_ref.shape[1]), jnp.float32)
    stores = []
    for start in range(0, width, column_chunk):
        cols = slice(start, start + column_chunk)
        wide = embedded_ref[:, cols].astype(jnp.float32)
        gain = jnp.concatenate(
            [
                gain_ref[row : row + 1, :]
                for row in range(start // 128, (start + column_chunk) // 128)
            ],
            axis=1,
        )
        normed = (wide * factor * gain.astype(jnp.float32)).astype(jnp.bfloat16)
        embedded_ref[:tokens, cols] = normed[:tokens]
        if (start + column_chunk) % piece_cols == 0:
            piece = start // piece_cols
            done = pl.ds(piece * piece_cols, piece_cols)
            stores.append(
                pltpu.make_async_copy(
                    embedded_ref.at[:tokens, done], normed_ref.at[:, done], out_sems.at[piece]
                )
            )
            stores[-1].start()
        summed += jnp.dot(normed, weight_ref[cols, :], preferred_element_type=jnp.float32)
    noisy_ref[...] = summed[:tokens].astype(jnp.bfloat16)
    swap = plan_ref[1:2, :] > 0.5
    clean_ref[:tokens, :] = swap_spans(summed[tokens:], swap).astype(jnp.bfloat16)
    first_row = lax.broadcasted_iota(jnp.int32, plan_ref.shape, 0) == 0
    clean_ref[tokens:, :] = jnp.where(first_row, plan_ref[...], 0.0).astype(jnp.bfloat16)
    for store in stores:
        store.wait()


def embed_tokens(
    plan, own_patches, other_patches, own_embed, other_embed, position, gain, weight
):
    tokens, width = position.shape
    vmem = pl.BlockSpec(memory_space=pltpu.VMEM)
    hbm = pl.BlockSpec(memory_space=pltpu.HBM)
    kv_shape = jax.ShapeDtypeStruct((tokens, weight.shape[1]), jnp.bfloat16)
    clean_shape = jax.ShapeDtypeStruct((tokens + meta_rows, weight.shape[1]), jnp.bfloat16)
    return pl.pallas_call(
        embed_kernel,
        out_shape=(pltpu.HBM((tokens, width), jnp.bfloat16), kv_shape, clean_shape),
        in_specs=[vmem, vmem, vmem, hbm, vmem, hbm, vmem, vmem],
        out_specs=(hbm, vmem, vmem),
        scratch_shapes=[
            pltpu.VMEM((2 * tokens, width), jnp.bfloat16),
            pltpu.VMEM(own_embed.shape, jnp.bfloat16),
            pltpu.VMEM(position.shape, jnp.bfloat16),
            pltpu.SemaphoreType.DMA((2, embed_pieces)),
            pltpu.SemaphoreType.DMA((embed_pieces,)),
        ],
        compiler_params=pltpu.CompilerParams(vmem_limit_bytes=24 * 1024 * 1024),
    )(
        plan,
        own_patches,
        other_patches,
        in_hbm(own_embed),
        other_embed,
        in_hbm(position),
        gain.reshape(-1, 128),
        weight,
    )


def on_device(
    clean_latents,
    noise,
    timesteps,
    span_order,
    valid_frames,
    embed_weight,
    position,
    norm_gain,
    query_weight,
    kv_weight,
):
    core = lax.axis_index("core")
    half = embed_weight.shape[0] // 2
    own_embed = lax.all_gather(
        lax.dynamic_slice_in_dim(embed_weight, core * half, half, 0), HEAD, axis=1, tiled=True
    )
    kv_cols = kv_weight.shape[1]
    q_cols = query_weight.shape[1]
    weights = jnp.concatenate([query_weight, kv_weight], axis=1).astype(jnp.float16)
    weights_pair = lax.all_gather(weights, "yh", axis=0)
    gathered = lax.all_gather(weights_pair, ("z", "core"), axis=1, tiled=True)
    gathered, own_embed = lax.optimization_barrier((gathered, own_embed))
    gathered = gathered.reshape(-1, q_cols + kv_cols)
    kv_full = gathered[:, q_cols:].astype(jnp.bfloat16)

    other_embed = lax.ppermute(own_embed, "core", [(0, 1), (1, 0)])
    own_patches, other_patches, plan = make_patches(
        timesteps, span_order, valid_frames, clean_latents, noise, own_embed
    )
    normed_noisy, noisy_kv, clean_kv = embed_tokens(
        plan,
        own_patches,
        other_patches,
        own_embed,
        other_embed,
        position,
        norm_gain,
        kv_full,
    )

    queries = jnp.dot(
        normed_noisy,
        gathered[:, :q_cols].astype(jnp.bfloat16),
        preferred_element_type=jnp.float32,
    ).astype(jnp.bfloat16)

    slots = span_order.shape[0]
    rows = clean_kv.shape[0]
    clean_pair = lax.all_gather(clean_kv.astype(jnp.float16), "yh", axis=0)
    clean_all = lax.all_gather(clean_pair, ("z", "core"), axis=1, tiled=True)
    clean_all = clean_all.reshape(-1, rows, kv_cols)
    meta_all = jnp.sum(clean_all[:, rows - meta_rows :, : 2 * slots].astype(jnp.float32), axis=1)
    return attention(
        span_order, valid_frames, queries, noisy_kv, clean_all.astype(jnp.bfloat16), meta_all
    )


def solution(mesh):
    fine = Mesh(mesh.devices.reshape(2, 16, 2, 4, 2), CTX + HEAD)
    return jax.shard_map(
        on_device,
        mesh=fine,
        in_specs=(
            P(CTX, None, None, None),
            P(CTX, None, None, None),
            P(CTX),
            P(CTX),
            P(CTX),
            P(None, HEAD),
            P(CTX, None),
            P(),
            P(CTX, HEAD),
            P(CTX, HEAD),
        ),
        out_specs=P(CTX, HEAD),
        check_vma=False,
    )
```

```python
import math

import jax
import jax.numpy as jnp
from jax import lax
from jax.experimental import pallas as pl
from jax.experimental.pallas import tpu as pltpu
from jax.sharding import Mesh, PartitionSpec as P

HD = 128
CH = 16


eps_norm = 1e-06
masked_low = -1e30


def in_hbm(array):
    return pltpu.with_memory_space_constraint(array, pltpu.HBM)


def ordered_spans(order_ref, valid_ref):
    swap = order_ref[0] > order_ref[1]
    orders = (jnp.minimum(order_ref[0], order_ref[1]), jnp.maximum(order_ref[0], order_ref[1]))
    valids = (
        jnp.where(swap, valid_ref[1], valid_ref[0]),
        jnp.where(swap, valid_ref[0], valid_ref[1]),
    )
    return swap, orders, valids


def swap_spans(values, swap):
    rows = values.shape[0] // 2
    turned = jnp.concatenate([values[rows:], values[:rows]], axis=0)
    return jnp.where(swap, turned, values)


def patch_kernel(
    time_ref,
    order_ref,
    valid_ref,
    clean_hbm,
    noise_hbm,
    after_ref,
    own_ref,
    other_ref,
    plan_ref,
    clean_ref,
    noise_ref,
    sems,
):
    del after_ref
    loads = [
        pltpu.make_async_copy(clean_hbm, clean_ref, sems.at[0]),
        pltpu.make_async_copy(noise_hbm, noise_ref, sems.at[1]),
    ]
    for load in loads:
        load.start()
    rows, lanes = clean_ref.shape
    row = lax.broadcasted_iota(jnp.int32, (rows, lanes), 0)
    steps = jnp.where(row < rows // 2, time_ref[0], time_ref[1])
    level = (steps.astype(jnp.float32) + 1.0) / 1000.0
    for load in loads:
        load.wait()
    clean = clean_ref[...]
    noisy = (
        (1.0 - level) * clean.astype(jnp.float32) + level * noise_ref[...].astype(jnp.float32)
    ).astype(jnp.bfloat16)
    latents = jnp.concatenate([noisy, clean], axis=0)
    count = 2 * rows
    source = lax.broadcasted_iota(jnp.int32, (lanes, 256), 0)
    target = lax.broadcasted_iota(jnp.int32, (lanes, 256), 1)
    token = lax.broadcasted_iota(jnp.int32, (256, 4 * count), 0)
    place = lax.broadcasted_iota(jnp.int32, (256, 4 * count), 1)
    result = jnp.zeros((256, 256), jnp.float32)
    for kernel_row in range(4):
        shifted = []
        for token_col in range(4):
            wanted = (target & 63) + (32 * token_col - 16)
            pick = (source == wanted) & ((target >> 6) == kernel_row)
            pick = jnp.where(pick, 1.0, 0.0).astype(jnp.bfloat16)
            shifted.append(
                jnp.dot(latents, pick, preferred_element_type=jnp.float32).astype(jnp.bfloat16)
            )
        latent_row = 2 * ((token >> 2) & 3) - 1 + kernel_row
        wanted = (token & 3) * count + (token >> 4) * 8 + latent_row
        pick = (place == wanted) & (latent_row >= 0) & (latent_row < 8)
        pick = jnp.where(pick, 1.0, 0.0).astype(jnp.bfloat16)
        result += jnp.dot(pick, jnp.concatenate(shifted, axis=0), preferred_element_type=jnp.float32)
    patches = result.astype(jnp.bfloat16)
    half = patches.shape[1] // 2
    upper = lax.axis_index("core") == 1
    own_ref[...] = jnp.where(upper, patches[:, half:], patches[:, :half])
    other_ref[...] = jnp.where(upper, patches[:, :half], patches[:, half:])
    swap, orders, valids = ordered_spans(order_ref, valid_ref)
    lane = lax.broadcasted_iota(jnp.int32, plan_ref.shape, 1)
    plan_row = lax.broadcasted_iota(jnp.int32, plan_ref.shape, 0)
    plan = jnp.where(plan_row == 1, jnp.where(swap, 1.0, 0.0), 0.0)
    for place, entry in enumerate(orders + valids):
        plan = jnp.where((plan_row == 0) & (lane == place), entry.astype(jnp.float32), plan)
    plan_ref[...] = plan


def make_patches(timesteps, order, valid, clean_latents, noise, after):
    smem = pl.BlockSpec(memory_space=pltpu.SMEM)
    flat = clean_latents.shape[-1]
    rows = clean_latents.size // flat
    hbm = pl.BlockSpec(memory_space=pltpu.HBM)
    vmem = pl.BlockSpec(memory_space=pltpu.VMEM)
    shape = jax.ShapeDtypeStruct((256, 128), jnp.bfloat16)
    return pl.pallas_call(
        patch_kernel,
        out_shape=(shape, shape, jax.ShapeDtypeStruct((meta_rows, 256), jnp.float32)),
        in_specs=[smem, smem, smem, hbm, hbm, hbm],
        out_specs=(vmem, vmem, vmem),
        scratch_shapes=[
            pltpu.VMEM((rows, flat), jnp.bfloat16),
            pltpu.VMEM((rows, flat), jnp.bfloat16),
            pltpu.SemaphoreType.DMA((2,)),
        ],
        compiler_params=pltpu.CompilerParams(vmem_limit_bytes=8 * 1024 * 1024),
    )(
        in_hbm(timesteps),
        in_hbm(order),
        in_hbm(valid),
        in_hbm(clean_latents.reshape(rows, flat)),
        in_hbm(noise.reshape(rows, flat)),
        in_hbm(after),
    )


CTX = ("yh", "z", "core")
HEAD = ("x", "yl")
meta_rows = 8
score_factor = HD ** (-0.5) * math.log2(math.e)
key_chunk = 2048
column_chunk = 768
embed_pieces = 4


def attention_kernel(
    order_ref, valid_ref, query_ref, own_ref, kv_ref, meta_ref, out_ref
):
    tokens = query_ref.shape[0]
    group = query_ref.shape[1] // HD
    span_rows = tokens // 2
    frame_rows = span_rows // 4
    chunk_blocks = key_chunk // span_rows
    chunks = kv_ref.shape[0] // chunk_blocks
    swap, orders, valids = ordered_spans(order_ref, valid_ref)
    queries = swap_spans(query_ref[...], swap)
    own = swap_spans(own_ref[...], swap)
    q = jnp.concatenate(
        [
            queries[slot * span_rows : (slot + 1) * span_rows, g * HD : (g + 1) * HD]
            for slot in range(2)
            for g in range(group)
        ],
        axis=0,
    )
    slot_rows = group * span_rows

    def scores_of(rows, keys):
        return lax.dot_general(
            rows, keys, (((1,), (1,)), ((), ())), preferred_element_type=jnp.float32
        )

    col = lax.broadcasted_iota(jnp.int32, (1, tokens), 1)
    states = []
    for slot in range(2):
        inside = (col >= slot * span_rows) & (
            col < slot * span_rows + valids[slot] * frame_rows
        )
        s = scores_of(q[slot * slot_rows : (slot + 1) * slot_rows], own[:, :HD]) * score_factor
        s += jnp.where(inside, 0.0, masked_low)
        largest = jnp.max(s, axis=1, keepdims=True)
        raw = jnp.exp2(s - largest)
        total = jnp.sum(raw, axis=1, keepdims=True)
        summed = jnp.dot(
            raw.astype(jnp.bfloat16), own[:, HD:], preferred_element_type=jnp.float32
        )
        states.append((largest, total, summed))

    def fold(state, s, values):
        largest, total, summed = state
        new_largest = jnp.maximum(largest, jnp.max(s, axis=1, keepdims=True))
        raw = jnp.exp2(s - new_largest)
        factor = jnp.exp2(largest - new_largest)
        total = total * factor + jnp.sum(raw, axis=1, keepdims=True)
        summed = summed * factor + jnp.dot(
            raw.astype(jnp.bfloat16), values, preferred_element_type=jnp.float32
        )
        return (new_largest, total, summed)

    block_row = lax.broadcasted_iota(jnp.int32, (chunk_blocks, key_chunk), 0)
    block_col = lax.broadcasted_iota(jnp.int32, (chunk_blocks, key_chunk), 1)
    pick = jnp.where(block_row == block_col // span_rows, 1.0, 0.0).astype(jnp.bfloat16)
    key_place = lax.broadcasted_iota(jnp.int32, (1, key_chunk), 1)
    key_frame = ((key_place & (span_rows - 1)) // frame_rows).astype(jnp.float32)
    limits = [order.astype(jnp.float32) for order in orders]
    for piece in range(chunks):
        part = slice(piece * chunk_blocks, (piece + 1) * chunk_blocks)
        spread = lax.dot_general(
            meta_ref[part, :].astype(jnp.bfloat16),
            pick,
            (((0,), (0,)), ((), ())),
            preferred_element_type=jnp.float32,
        )
        for key_slot in range(2):
            block = kv_ref[part, key_slot * span_rows : (key_slot + 1) * span_rows, :]
            block = block.reshape(key_chunk, 2 * HD)
            key_order = spread[key_slot : key_slot + 1]
            live = key_frame < spread[2 + key_slot : 3 + key_slot]
            s = scores_of(q[key_slot * slot_rows :], block[:, :HD]) * score_factor
            for slot in range(key_slot, 2):
                bias = jnp.where(live & (key_order < limits[slot]), 0.0, masked_low)
                begin = (slot - key_slot) * slot_rows
                states[slot] = fold(
                    states[slot], s[begin : begin + slot_rows] + bias, block[:, HD:]
                )

    token = lax.broadcasted_iota(jnp.int32, (span_rows, HD), 0)
    pieces = []
    for slot in range(2):
        largest, total, summed = states[slot]
        result = summed / total
        live_row = token < valids[slot] * frame_rows
        pieces.append(
            jnp.concatenate(
                [
                    jnp.where(live_row, result[g * span_rows : (g + 1) * span_rows], 0.0)
                    for g in range(group)
                ],
                axis=1,
            )
        )
    out_ref[...] = swap_spans(jnp.concatenate(pieces, axis=0), swap).astype(jnp.bfloat16)


def attention(order, valid, queries, own, kv_all, meta):
    smem = pl.BlockSpec(memory_space=pltpu.SMEM)
    vmem = pl.BlockSpec(memory_space=pltpu.VMEM)
    return pl.pallas_call(
        attention_kernel,
        out_shape=jax.ShapeDtypeStruct(queries.shape, jnp.bfloat16),
        in_specs=[smem, smem, vmem, vmem, vmem, vmem],
        out_specs=vmem,
        compiler_params=pltpu.CompilerParams(vmem_limit_bytes=16 * 1024 * 1024),
    )(in_hbm(order), in_hbm(valid), queries, own, kv_all, meta)


def embed_kernel(
    plan_ref,
    own_patch_ref,
    other_patch_ref,
    own_embed_ref,
    other_embed_ref,
    position_ref,
    gain_ref,
    weight_ref,
    normed_ref,
    noisy_ref,
    clean_ref,
    embedded_ref,
    own_buffer,
    position_buffer,
    sems,
    out_sems,
):
    tokens, width = position_ref.shape
    piece_cols = width // embed_pieces
    copies = []
    for piece in range(embed_pieces):
        cols = pl.ds(piece * piece_cols, piece_cols)
        for index, (source, buffer) in enumerate(
            (
                (own_embed_ref, own_buffer),
                (position_ref, position_buffer),
            )
        ):
            copies.append(
                pltpu.make_async_copy(source.at[:, cols], buffer.at[:, cols], sems.at[index, piece])
            )
            copies[-1].start()
    patches = jnp.concatenate([own_patch_ref[...], other_patch_ref[...]], axis=1)
    squares = jnp.zeros((2 * tokens, 128), jnp.float32)
    for start in range(0, width, column_chunk):
        cols = slice(start, start + column_chunk)
        if start % piece_cols == 0:
            first = 2 * (start // piece_cols)
            for copy in copies[first : first + 2]:
                copy.wait()
        embed = jnp.concatenate([own_buffer[:, cols], other_embed_ref[:, cols]], axis=0)
        projected = jnp.dot(patches, embed, preferred_element_type=jnp.float32)
        place = position_buffer[:, cols].astype(jnp.float32)
        embedded = (projected + jnp.concatenate([place, place], axis=0)).astype(jnp.bfloat16)
        embedded_ref[:, cols] = embedded
        wide = embedded.astype(jnp.float32)
        for lane in range(0, column_chunk, 128):
            squares += wide[:, lane : lane + 128] * wide[:, lane : lane + 128]
    factor = lax.rsqrt(jnp.sum(squares, axis=1, keepdims=True) / width + eps_norm)
    summed = jnp.zeros((2 * tokens, weight_ref.shape[1]), jnp.float32)
    stores = []
    for start in range(0, width, column_chunk):
        cols = slice(start, start + column_chunk)
        wide = embedded_ref[:, cols].astype(jnp.float32)
        gain = jnp.concatenate(
            [
                gain_ref[row : row + 1, :]
                for row in range(start // 128, (start + column_chunk) // 128)
            ],
            axis=1,
        )
        normed = (wide * factor * gain.astype(jnp.float32)).astype(jnp.bfloat16)
        embedded_ref[:tokens, cols] = normed[:tokens]
        if (start + column_chunk) % piece_cols == 0:
            piece = start // piece_cols
            done = pl.ds(piece * piece_cols, piece_cols)
            stores.append(
                pltpu.make_async_copy(
                    embedded_ref.at[:tokens, done], normed_ref.at[:, done], out_sems.at[piece]
                )
            )
            stores[-1].start()
        summed += jnp.dot(normed, weight_ref[cols, :], preferred_element_type=jnp.float32)
    noisy_ref[...] = summed[:tokens].astype(jnp.bfloat16)
    swap = plan_ref[1:2, :] > 0.5
    clean_ref[:tokens, :] = swap_spans(summed[tokens:], swap).astype(jnp.bfloat16)
    first_row = lax.broadcasted_iota(jnp.int32, plan_ref.shape, 0) == 0
    clean_ref[tokens:, :] = jnp.where(first_row, plan_ref[...], 0.0).astype(jnp.bfloat16)
    for store in stores:
        store.wait()


def embed_tokens(
    plan, own_patches, other_patches, own_embed, other_embed, position, gain, weight
):
    tokens, width = position.shape
    vmem = pl.BlockSpec(memory_space=pltpu.VMEM)
    hbm = pl.BlockSpec(memory_space=pltpu.HBM)
    kv_shape = jax.ShapeDtypeStruct((tokens, weight.shape[1]), jnp.bfloat16)
    clean_shape = jax.ShapeDtypeStruct((tokens + meta_rows, weight.shape[1]), jnp.bfloat16)
    return pl.pallas_call(
        embed_kernel,
        out_shape=(pltpu.HBM((tokens, width), jnp.bfloat16), kv_shape, clean_shape),
        in_specs=[vmem, vmem, vmem, hbm, vmem, hbm, vmem, vmem],
        out_specs=(hbm, vmem, vmem),
        scratch_shapes=[
            pltpu.VMEM((2 * tokens, width), jnp.bfloat16),
            pltpu.VMEM(own_embed.shape, jnp.bfloat16),
            pltpu.VMEM(position.shape, jnp.bfloat16),
            pltpu.SemaphoreType.DMA((2, embed_pieces)),
            pltpu.SemaphoreType.DMA((embed_pieces,)),
        ],
        compiler_params=pltpu.CompilerParams(vmem_limit_bytes=24 * 1024 * 1024),
    )(
        plan,
        own_patches,
        other_patches,
        in_hbm(own_embed),
        other_embed,
        in_hbm(position),
        gain.reshape(-1, 128),
        weight,
    )


def on_device(
    clean_latents,
    noise,
    timesteps,
    span_order,
    valid_frames,
    embed_weight,
    position,
    norm_gain,
    query_weight,
    kv_weight,
):
    core = lax.axis_index("core")
    half = embed_weight.shape[0] // 2
    own_embed = lax.all_gather(
        lax.dynamic_slice_in_dim(embed_weight, core * half, half, 0), HEAD, axis=1, tiled=True
    )
    kv_cols = kv_weight.shape[1]
    q_cols = query_weight.shape[1]
    weights = jnp.concatenate([query_weight, kv_weight], axis=1).astype(jnp.float16)
    weights_pair = lax.all_gather(weights, "yh", axis=0)
    gathered = lax.all_gather(weights_pair, ("z", "core"), axis=1, tiled=True)
    gathered, own_embed = lax.optimization_barrier((gathered, own_embed))
    gathered = gathered.reshape(-1, q_cols + kv_cols)
    kv_full = gathered[:, q_cols:].astype(jnp.bfloat16)

    other_embed = lax.ppermute(own_embed, "core", [(0, 1), (1, 0)])
    own_patches, other_patches, plan = make_patches(
        timesteps, span_order, valid_frames, clean_latents, noise, own_embed
    )
    normed_noisy, noisy_kv, clean_kv = embed_tokens(
        plan,
        own_patches,
        other_patches,
        own_embed,
        other_embed,
        position,
        norm_gain,
        kv_full,
    )

    queries = jnp.dot(
        normed_noisy,
        gathered[:, :q_cols].astype(jnp.bfloat16),
        preferred_element_type=jnp.float32,
    ).astype(jnp.bfloat16)

    slots = span_order.shape[0]
    rows = clean_kv.shape[0]
    clean_pair = lax.all_gather(clean_kv.astype(jnp.float16), "yh", axis=0)
    clean_all = lax.all_gather(clean_pair, ("z", "core"), axis=1, tiled=True)
    clean_all = clean_all.reshape(-1, rows, kv_cols)
    meta_all = jnp.sum(clean_all[:, rows - meta_rows :, : 2 * slots].astype(jnp.float32), axis=1)
    return attention(
        span_order, valid_frames, queries, noisy_kv, clean_all.astype(jnp.bfloat16), meta_all
    )


def solution(mesh):
    fine = Mesh(mesh.devices.reshape(2, 16, 2, 4, 2), CTX + HEAD)
    return jax.shard_map(
        on_device,
        mesh=fine,
        in_specs=(
            P(CTX, None, None, None),
            P(CTX, None, None, None),
            P(CTX),
            P(CTX),
            P(CTX),
            P(None, HEAD),
            P(CTX, None),
            P(),
            P(CTX, HEAD),
            P(CTX, HEAD),
        ),
        out_specs=P(CTX, HEAD),
        check_vma=False,
    )
```

```python
import math

import jax
import jax.numpy as jnp
from jax import lax
from jax.experimental import pallas as pl
from jax.experimental.pallas import tpu as pltpu
from jax.sharding import Mesh, PartitionSpec as P

HD = 128
CH = 16


eps_norm = 1e-06
masked_low = -1e30


def in_hbm(array):
    return pltpu.with_memory_space_constraint(array, pltpu.HBM)


def ordered_spans(order_ref, valid_ref):
    swap = order_ref[0] > order_ref[1]
    orders = (jnp.minimum(order_ref[0], order_ref[1]), jnp.maximum(order_ref[0], order_ref[1]))
    valids = (
        jnp.where(swap, valid_ref[1], valid_ref[0]),
        jnp.where(swap, valid_ref[0], valid_ref[1]),
    )
    return swap, orders, valids


def swap_spans(values, swap):
    rows = values.shape[0] // 2
    turned = jnp.concatenate([values[rows:], values[:rows]], axis=0)
    return jnp.where(swap, turned, values)


def patch_kernel(
    time_ref,
    order_ref,
    valid_ref,
    clean_hbm,
    noise_hbm,
    after_ref,
    own_ref,
    other_ref,
    plan_ref,
    clean_ref,
    noise_ref,
    sems,
):
    del after_ref
    loads = [
        pltpu.make_async_copy(clean_hbm, clean_ref, sems.at[0]),
        pltpu.make_async_copy(noise_hbm, noise_ref, sems.at[1]),
    ]
    for load in loads:
        load.start()
    rows, lanes = clean_ref.shape
    row = lax.broadcasted_iota(jnp.int32, (rows, lanes), 0)
    steps = jnp.where(row < rows // 2, time_ref[0], time_ref[1])
    level = (steps.astype(jnp.float32) + 1.0) / 1000.0
    for load in loads:
        load.wait()
    clean = clean_ref[...]
    noisy = (
        (1.0 - level) * clean.astype(jnp.float32) + level * noise_ref[...].astype(jnp.float32)
    ).astype(jnp.bfloat16)
    latents = jnp.concatenate([noisy, clean], axis=0)
    count = 2 * rows
    source = lax.broadcasted_iota(jnp.int32, (lanes, 256), 0)
    target = lax.broadcasted_iota(jnp.int32, (lanes, 256), 1)
    token = lax.broadcasted_iota(jnp.int32, (256, 4 * count), 0)
    place = lax.broadcasted_iota(jnp.int32, (256, 4 * count), 1)
    result = jnp.zeros((256, 256), jnp.float32)
    for kernel_row in range(4):
        shifted = []
        for token_col in range(4):
            wanted = (target & 63) + (32 * token_col - 16)
            pick = (source == wanted) & ((target >> 6) == kernel_row)
            pick = jnp.where(pick, 1.0, 0.0).astype(jnp.bfloat16)
            shifted.append(
                jnp.dot(latents, pick, preferred_element_type=jnp.float32).astype(jnp.bfloat16)
            )
        latent_row = 2 * ((token >> 2) & 3) - 1 + kernel_row
        wanted = (token & 3) * count + (token >> 4) * 8 + latent_row
        pick = (place == wanted) & (latent_row >= 0) & (latent_row < 8)
        pick = jnp.where(pick, 1.0, 0.0).astype(jnp.bfloat16)
        result += jnp.dot(pick, jnp.concatenate(shifted, axis=0), preferred_element_type=jnp.float32)
    patches = result.astype(jnp.bfloat16)
    half = patches.shape[1] // 2
    upper = lax.axis_index("core") == 1
    own_ref[...] = jnp.where(upper, patches[:, half:], patches[:, :half])
    other_ref[...] = jnp.where(upper, patches[:, :half], patches[:, half:])
    swap, orders, valids = ordered_spans(order_ref, valid_ref)
    lane = lax.broadcasted_iota(jnp.int32, plan_ref.shape, 1)
    plan_row = lax.broadcasted_iota(jnp.int32, plan_ref.shape, 0)
    plan = jnp.where(plan_row == 1, jnp.where(swap, 1.0, 0.0), 0.0)
    for place, entry in enumerate(orders + valids):
        plan = jnp.where((plan_row == 0) & (lane == place), entry.astype(jnp.float32), plan)
    plan_ref[...] = plan


def make_patches(timesteps, order, valid, clean_latents, noise, after):
    smem = pl.BlockSpec(memory_space=pltpu.SMEM)
    flat = clean_latents.shape[-1]
    rows = clean_latents.size // flat
    hbm = pl.BlockSpec(memory_space=pltpu.HBM)
    vmem = pl.BlockSpec(memory_space=pltpu.VMEM)
    shape = jax.ShapeDtypeStruct((256, 128), jnp.bfloat16)
    return pl.pallas_call(
        patch_kernel,
        out_shape=(shape, shape, jax.ShapeDtypeStruct((meta_rows, 256), jnp.float32)),
        in_specs=[smem, smem, smem, hbm, hbm, hbm],
        out_specs=(vmem, vmem, vmem),
        scratch_shapes=[
            pltpu.VMEM((rows, flat), jnp.bfloat16),
            pltpu.VMEM((rows, flat), jnp.bfloat16),
            pltpu.SemaphoreType.DMA((2,)),
        ],
        compiler_params=pltpu.CompilerParams(vmem_limit_bytes=8 * 1024 * 1024),
    )(
        in_hbm(timesteps),
        in_hbm(order),
        in_hbm(valid),
        in_hbm(clean_latents.reshape(rows, flat)),
        in_hbm(noise.reshape(rows, flat)),
        in_hbm(after),
    )


CTX = ("yh", "z", "core")
HEAD = ("x", "yl")
meta_rows = 8
score_factor = HD ** (-0.5) * math.log2(math.e)
key_chunk = 2048
column_chunk = 1536
embed_pieces = 4


def attention_kernel(
    order_ref, valid_ref, query_ref, own_ref, kv_ref, meta_ref, out_ref
):
    tokens = query_ref.shape[0]
    group = query_ref.shape[1] // HD
    span_rows = tokens // 2
    frame_rows = span_rows // 4
    chunk_blocks = key_chunk // span_rows
    chunks = kv_ref.shape[0] // chunk_blocks
    swap, orders, valids = ordered_spans(order_ref, valid_ref)
    queries = swap_spans(query_ref[...], swap)
    own = swap_spans(own_ref[...], swap)
    q = jnp.concatenate(
        [
            queries[slot * span_rows : (slot + 1) * span_rows, g * HD : (g + 1) * HD]
            for slot in range(2)
            for g in range(group)
        ],
        axis=0,
    )
    slot_rows = group * span_rows

    def scores_of(rows, keys):
        return lax.dot_general(
            rows, keys, (((1,), (1,)), ((), ())), preferred_element_type=jnp.float32
        )

    col = lax.broadcasted_iota(jnp.int32, (1, tokens), 1)
    states = []
    for slot in range(2):
        inside = (col >= slot * span_rows) & (
            col < slot * span_rows + valids[slot] * frame_rows
        )
        s = scores_of(q[slot * slot_rows : (slot + 1) * slot_rows], own[:, :HD]) * score_factor
        s += jnp.where(inside, 0.0, masked_low)
        largest = jnp.max(s, axis=1, keepdims=True)
        raw = jnp.exp2(s - largest)
        total = jnp.sum(raw, axis=1, keepdims=True)
        summed = jnp.dot(
            raw.astype(jnp.bfloat16), own[:, HD:], preferred_element_type=jnp.float32
        )
        states.append((largest, total, summed))

    def fold(state, s, values):
        largest, total, summed = state
        new_largest = jnp.maximum(largest, jnp.max(s, axis=1, keepdims=True))
        raw = jnp.exp2(s - new_largest)
        factor = jnp.exp2(largest - new_largest)
        total = total * factor + jnp.sum(raw, axis=1, keepdims=True)
        summed = summed * factor + jnp.dot(
            raw.astype(jnp.bfloat16), values, preferred_element_type=jnp.float32
        )
        return (new_largest, total, summed)

    block_row = lax.broadcasted_iota(jnp.int32, (chunk_blocks, key_chunk), 0)
    block_col = lax.broadcasted_iota(jnp.int32, (chunk_blocks, key_chunk), 1)
    pick = jnp.where(block_row == block_col // span_rows, 1.0, 0.0).astype(jnp.bfloat16)
    key_place = lax.broadcasted_iota(jnp.int32, (1, key_chunk), 1)
    key_frame = ((key_place & (span_rows - 1)) // frame_rows).astype(jnp.float32)
    limits = [order.astype(jnp.float32) for order in orders]
    for piece in range(chunks):
        part = slice(piece * chunk_blocks, (piece + 1) * chunk_blocks)
        spread = lax.dot_general(
            meta_ref[part, :].astype(jnp.bfloat16),
            pick,
            (((0,), (0,)), ((), ())),
            preferred_element_type=jnp.float32,
        )
        for key_slot in range(2):
            block = kv_ref[part, key_slot * span_rows : (key_slot + 1) * span_rows, :]
            block = block.reshape(key_chunk, 2 * HD)
            key_order = spread[key_slot : key_slot + 1]
            live = key_frame < spread[2 + key_slot : 3 + key_slot]
            s = scores_of(q[key_slot * slot_rows :], block[:, :HD]) * score_factor
            for slot in range(key_slot, 2):
                bias = jnp.where(live & (key_order < limits[slot]), 0.0, masked_low)
                begin = (slot - key_slot) * slot_rows
                states[slot] = fold(
                    states[slot], s[begin : begin + slot_rows] + bias, block[:, HD:]
                )

    token = lax.broadcasted_iota(jnp.int32, (span_rows, HD), 0)
    pieces = []
    for slot in range(2):
        largest, total, summed = states[slot]
        result = summed / total
        live_row = token < valids[slot] * frame_rows
        pieces.append(
            jnp.concatenate(
                [
                    jnp.where(live_row, result[g * span_rows : (g + 1) * span_rows], 0.0)
                    for g in range(group)
                ],
                axis=1,
            )
        )
    out_ref[...] = swap_spans(jnp.concatenate(pieces, axis=0), swap).astype(jnp.bfloat16)


def attention(order, valid, queries, own, kv_all, meta):
    smem = pl.BlockSpec(memory_space=pltpu.SMEM)
    vmem = pl.BlockSpec(memory_space=pltpu.VMEM)
    return pl.pallas_call(
        attention_kernel,
        out_shape=jax.ShapeDtypeStruct(queries.shape, jnp.bfloat16),
        in_specs=[smem, smem, vmem, vmem, vmem, vmem],
        out_specs=vmem,
        compiler_params=pltpu.CompilerParams(vmem_limit_bytes=16 * 1024 * 1024),
    )(in_hbm(order), in_hbm(valid), queries, own, kv_all, meta)


def embed_kernel(
    plan_ref,
    own_patch_ref,
    other_patch_ref,
    own_embed_ref,
    other_embed_ref,
    position_ref,
    gain_ref,
    weight_ref,
    normed_ref,
    noisy_ref,
    clean_ref,
    embedded_ref,
    own_buffer,
    position_buffer,
    sems,
    out_sems,
):
    tokens, width = position_ref.shape
    piece_cols = width // embed_pieces
    copies = []
    for piece in range(embed_pieces):
        cols = pl.ds(piece * piece_cols, piece_cols)
        for index, (source, buffer) in enumerate(
            (
                (own_embed_ref, own_buffer),
                (position_ref, position_buffer),
            )
        ):
            copies.append(
                pltpu.make_async_copy(source.at[:, cols], buffer.at[:, cols], sems.at[index, piece])
            )
            copies[-1].start()
    patches = jnp.concatenate([own_patch_ref[...], other_patch_ref[...]], axis=1)
    squares = jnp.zeros((2 * tokens, 128), jnp.float32)
    for start in range(0, width, column_chunk):
        cols = slice(start, start + column_chunk)
        if start % piece_cols == 0:
            first = 2 * (start // piece_cols)
            for copy in copies[first : first + 2]:
                copy.wait()
        embed = jnp.concatenate([own_buffer[:, cols], other_embed_ref[:, cols]], axis=0)
        projected = jnp.dot(patches, embed, preferred_element_type=jnp.float32)
        place = position_buffer[:, cols].astype(jnp.float32)
        embedded = (projected + jnp.concatenate([place, place], axis=0)).astype(jnp.bfloat16)
        embedded_ref[:, cols] = embedded
        wide = embedded.astype(jnp.float32)
        for lane in range(0, column_chunk, 128):
            squares += wide[:, lane : lane + 128] * wide[:, lane : lane + 128]
    factor = lax.rsqrt(jnp.sum(squares, axis=1, keepdims=True) / width + eps_norm)
    summed = jnp.zeros((2 * tokens, weight_ref.shape[1]), jnp.float32)
    stores = []
    for start in range(0, width, column_chunk):
        cols = slice(start, start + column_chunk)
        wide = embedded_ref[:, cols].astype(jnp.float32)
        gain = jnp.concatenate(
            [
                gain_ref[row : row + 1, :]
                for row in range(start // 128, (start + column_chunk) // 128)
            ],
            axis=1,
        )
        normed = (wide * factor * gain.astype(jnp.float32)).astype(jnp.bfloat16)
        embedded_ref[:tokens, cols] = normed[:tokens]
        if (start + column_chunk) % piece_cols == 0:
            piece = start // piece_cols
            done = pl.ds(piece * piece_cols, piece_cols)
            stores.append(
                pltpu.make_async_copy(
                    embedded_ref.at[:tokens, done], normed_ref.at[:, done], out_sems.at[piece]
                )
            )
            stores[-1].start()
        summed += jnp.dot(normed, weight_ref[cols, :], preferred_element_type=jnp.float32)
    noisy_ref[...] = summed[:tokens].astype(jnp.bfloat16)
    swap = plan_ref[1:2, :] > 0.5
    clean_ref[:tokens, :] = swap_spans(summed[tokens:], swap).astype(jnp.bfloat16)
    first_row = lax.broadcasted_iota(jnp.int32, plan_ref.shape, 0) == 0
    clean_ref[tokens:, :] = jnp.where(first_row, plan_ref[...], 0.0).astype(jnp.bfloat16)
    for store in stores:
        store.wait()


def embed_tokens(
    plan, own_patches, other_patches, own_embed, other_embed, position, gain, weight
):
    tokens, width = position.shape
    vmem = pl.BlockSpec(memory_space=pltpu.VMEM)
    hbm = pl.BlockSpec(memory_space=pltpu.HBM)
    kv_shape = jax.ShapeDtypeStruct((tokens, weight.shape[1]), jnp.bfloat16)
    clean_shape = jax.ShapeDtypeStruct((tokens + meta_rows, weight.shape[1]), jnp.bfloat16)
    return pl.pallas_call(
        embed_kernel,
        out_shape=(pltpu.HBM((tokens, width), jnp.bfloat16), kv_shape, clean_shape),
        in_specs=[vmem, vmem, vmem, hbm, vmem, hbm, vmem, vmem],
        out_specs=(hbm, vmem, vmem),
        scratch_shapes=[
            pltpu.VMEM((2 * tokens, width), jnp.bfloat16),
            pltpu.VMEM(own_embed.shape, jnp.bfloat16),
            pltpu.VMEM(position.shape, jnp.bfloat16),
            pltpu.SemaphoreType.DMA((2, embed_pieces)),
            pltpu.SemaphoreType.DMA((embed_pieces,)),
        ],
        compiler_params=pltpu.CompilerParams(vmem_limit_bytes=24 * 1024 * 1024),
    )(
        plan,
        own_patches,
        other_patches,
        in_hbm(own_embed),
        other_embed,
        in_hbm(position),
        gain.reshape(-1, 128),
        weight,
    )


def on_device(
    clean_latents,
    noise,
    timesteps,
    span_order,
    valid_frames,
    embed_weight,
    position,
    norm_gain,
    query_weight,
    kv_weight,
):
    core = lax.axis_index("core")
    half = embed_weight.shape[0] // 2
    own_embed = lax.all_gather(
        lax.dynamic_slice_in_dim(embed_weight, core * half, half, 0), HEAD, axis=1, tiled=True
    )
    kv_cols = kv_weight.shape[1]
    q_cols = query_weight.shape[1]
    weights = jnp.concatenate([query_weight, kv_weight], axis=1).astype(jnp.float16)
    weights_pair = lax.all_gather(weights, "yh", axis=0)
    gathered = lax.all_gather(weights_pair, ("z", "core"), axis=1, tiled=True)
    gathered, own_embed = lax.optimization_barrier((gathered, own_embed))
    gathered = gathered.reshape(-1, q_cols + kv_cols)
    kv_full = gathered[:, q_cols:].astype(jnp.bfloat16)

    other_embed = lax.ppermute(own_embed, "core", [(0, 1), (1, 0)])
    own_patches, other_patches, plan = make_patches(
        timesteps, span_order, valid_frames, clean_latents, noise, own_embed
    )
    normed_noisy, noisy_kv, clean_kv = embed_tokens(
        plan,
        own_patches,
        other_patches,
        own_embed,
        other_embed,
        position,
        norm_gain,
        kv_full,
    )

    queries = jnp.dot(
        normed_noisy,
        gathered[:, :q_cols].astype(jnp.bfloat16),
        preferred_element_type=jnp.float32,
    ).astype(jnp.bfloat16)

    slots = span_order.shape[0]
    rows = clean_kv.shape[0]
    clean_pair = lax.all_gather(clean_kv.astype(jnp.float16), "yh", axis=0)
    clean_all = lax.all_gather(clean_pair, ("z", "core"), axis=1, tiled=True)
    clean_all = clean_all.reshape(-1, rows, kv_cols)
    meta_all = jnp.sum(clean_all[:, rows - meta_rows :, : 2 * slots].astype(jnp.float32), axis=1)
    return attention(
        span_order, valid_frames, queries, noisy_kv, clean_all.astype(jnp.bfloat16), meta_all
    )


def solution(mesh):
    fine = Mesh(mesh.devices.reshape(2, 16, 2, 4, 2), CTX + HEAD)
    return jax.shard_map(
        on_device,
        mesh=fine,
        in_specs=(
            P(CTX, None, None, None),
            P(CTX, None, None, None),
            P(CTX),
            P(CTX),
            P(CTX),
            P(None, HEAD),
            P(CTX, None),
            P(),
            P(CTX, HEAD),
            P(CTX, HEAD),
        ),
        out_specs=P(CTX, HEAD),
        check_vma=False,
    )
```
